512 devices in a mesh: dp: 8 (over z_hi, core), expert: 64 (over x, z_lo, y).
Axes of the slice: x: 4, y: 4, z: 16 (z_hi: 4, z_lo: 4; z = z_hi * 4 + z_lo), core: 2. Of those that a mesh axis runs over, the one named last changes fastest.
Arguments:
- tokens: bfloat16 [98304, 1024], P(('dp', 'expert')), may hold values from -6 to 6
- out_grad: bfloat16 [98304, 1024], P(('dp', 'expert')), may hold values from -2.5 to 2.5
- gates: bfloat16 [98304, 2], P(('dp', 'expert')), may hold values from 0.099609375 to 0.8984375
- expert_ids: int32 [98304, 2], P(('dp', 'expert')), may hold values from 0 to 63, all different within a row; in each aligned block of 192 rows (0 to 191, 192 to 383, ...) at most 9 rows name the same one
- w_in: bfloat16 [64, 1024, 1024], P('expert', None, 'dp'), may hold values from -0.1875 to 0.1875
- w_out: bfloat16 [64, 1024, 1024], P('expert', None, 'dp'), may hold values from -0.1875 to 0.1875
Outputs:
- d_tokens: bfloat16 [98304, 1024], P(('dp', 'expert'))
- gate_grad: bfloat16 [98304, 2], P(('dp', 'expert'))
- grad_in: float32 [64, 1024, 1024], P('expert', None, 'dp')
- grad_out: float32 [64, 1024, 1024], P('expert', None, 'dp')
The draws below stay inside these ranges and needn't reach their ends.
Inputs may be any that keep to these rules, and one draw needn't show every extreme that they name: `expert_ids`: each row names two different experts. Among the 192 rows of one device no expert is named more than 9 times, and in every draw some device names some expert exactly 9 times.
All inputs are finite; a program needn't handle non-finite values.
Results may differ from the reference program's by a relative error of at most 0.022.
Values may be sent and summed in bfloat16 or wider, within the bound.
No kernel may reach another device: no remote copies, remote signals or barrier semaphores. Data moves between devices by JAX's collectives and lax.ppermute only.
A program may use at most 64 MiB of HBM per device.

```python
import math
import jax
import jax.numpy as jnp
import numpy as np
from jax import lax

D = 1024
FF = 1024
TOK_DEV = 192
EXPERTS = 64
CAP = 9
ROWS = 576
TOKEN_TOTAL = 98304
N_DP = 8
N_EXPERT = 64


def block_levels(own_key, dims, split, smallest, largest):
    def one(dim, blocks):
        steps = jax.random.uniform(jax.random.fold_in(jax.random.fold_in(own_key, 6), dim), (blocks,), jnp.float32, smallest / len(split), largest / len(split))
        return jnp.repeat(jnp.exp(steps), dims[dim] // blocks).reshape((-1,) + (1,) * (len(dims) - dim - 1))

    level = one(*split[0])
    for cut in split[1:]:
        level = level * one(*cut)
    return level


def shared_out(key, own, number, rows, count, top, limit, slope):
    order = jax.random.permutation(key, count)
    crowded, ordinary = load_shares(count, rows * top, limit, slope, True), load_shares(count, rows * top, limit, slope, False)
    places = jnp.arange(count)

    def named(tallies, rotation):
        used = int((tallies > 0).sum())
        fixed = max(1, used // 4)
        moved = fixed + (places - fixed + rotation * (used - fixed)) % max(1, count - fixed)
        return jnp.zeros((count,), jnp.int32).at[order[jnp.where(places < fixed, places, moved)]].set(jnp.asarray(tallies, jnp.int32))

    tallies = jnp.where(number % 4 == 0, named(crowded, number // 4), named(ordinary, number - number // 4 - 1))
    mixed = jax.random.permutation(jax.random.fold_in(own, 3), count)
    giver, sink = mixed[0:count // 2 * 2:2], mixed[1:count // 2 * 2:2]
    slack = jnp.minimum(tallies[giver] - 1, limit - tallies[sink]) // 2
    slack = jnp.where((giver == order[0]) | (sink == order[0]) | (tallies[sink] == 0), 0, jnp.maximum(slack, 0))
    moved = jax.random.randint(jax.random.fold_in(own, 4), (count // 2,), 0, 1 << 20) % (slack + 1)
    tallies = tallies.at[giver].add(-moved).at[sink].add(moved)
    members = jnp.searchsorted(jnp.cumsum(tallies), jnp.arange(rows * top), side="right").astype(jnp.int32)
    grid = members.reshape(top, rows).T
    grid = grid[jax.random.permutation(jax.random.fold_in(own, 1), rows)]
    rotation = jax.random.randint(jax.random.fold_in(own, 2), (rows, 1), 0, top)
    return jnp.take_along_axis(grid, (jnp.arange(top)[None, :] + rotation) % top, axis=1)


def load_shares(amount, total, limit, lean, full):
    portions = [(1 << 20) // math.isqrt(rank ** lean) + 1 for rank in range(1, amount + 1)]
    largest = limit if full else min(limit, max(-(-total // amount), total * portions[0] // sum(portions)))
    least = 1 if total - largest >= amount - 1 else 0
    given, spare = [largest] + [least] * (amount - 1), total - largest - least * (amount - 1)
    while spare > 0:
        movable = [i for i in range(1, amount) if given[i] < largest] or [i for i in range(1, amount) if given[i] < limit]
        mass, budget = sum([portions[i] for i in movable]), spare
        for i in movable:
            addition = min(limit - given[i], max(1, budget * portions[i] // mass), spare)
            given[i] = given[i] + addition
            spare = spare - addition
    return np.array(given)


def scatter_about(own_key, extent, deviation, limit, shards=(), kind=jnp.bfloat16):
    values = deviation * jax.random.normal(own_key, extent, jnp.float32)
    if shards:
        values = values * block_levels(own_key, extent, shards, -0.22, 0.18)
    return jnp.clip(values, -limit, limit).astype(kind)


def setup_inputs(seed: int = 0) -> dict:
    key_of = jax.random.split(jax.random.key(seed), 7)
    tokens = scatter_about(key_of[0], (TOKEN_TOTAL, D), 1.0, 6.0, ((0, 512),))
    out_grad = scatter_about(key_of[1], (TOKEN_TOTAL, D), 0.3, 2.5, ((0, 512),))
    gates = jnp.clip(0.099609375 + 0.7988281 * jax.random.uniform(key_of[2], (TOKEN_TOTAL, 2), jnp.float32) ** block_levels(key_of[2], (TOKEN_TOTAL, 2), ((0, 512),), -0.2, 0.2), 0.099609375, 0.8984375).astype(jnp.bfloat16)
    expert_ids_keys = jax.random.split(jax.random.fold_in(key_of[3], 1), TOKEN_TOTAL // TOK_DEV)
    expert_ids_turns = jax.random.permutation(jax.random.fold_in(key_of[3], 3), TOKEN_TOTAL // TOK_DEV)
    expert_ids = jax.vmap(lambda own, number: shared_out(jax.random.fold_in(key_of[3], 2), own, number, TOK_DEV, EXPERTS, 2, CAP, 0))(expert_ids_keys, expert_ids_turns).reshape((TOKEN_TOTAL, 2))
    w_in = scatter_about(key_of[4], (EXPERTS, D, FF), D ** -0.5, 0.1875, ((0, 64), (2, 8)))
    w_out = scatter_about(key_of[5], (EXPERTS, D, FF), FF ** -0.5, 0.1875, ((0, 64), (2, 8)))
    return {"tokens": tokens, "out_grad": out_grad, "gates": gates, "expert_ids": expert_ids, "w_in": w_in, "w_out": w_out}


gelu_scale = 0.7978845608028654
cubic_coef = 0.044715


def gelu_value(values):
    return 0.5 * values * (1.0 + jnp.tanh(gelu_scale * (values + cubic_coef * values * values * values)))


def gelu_slope(values):
    tanh_inner = jnp.tanh(gelu_scale * (values + cubic_coef * values * values * values))
    return 0.5 * (1.0 + tanh_inner) + 0.5 * values * (1.0 - tanh_inner * tanh_inner) * gelu_scale * (1.0 + 3.0 * cubic_coef * values * values)


def slot_positions(id_block):
    flat_ids = id_block.reshape(-1)
    onehot = (flat_ids[:, None] == jnp.arange(EXPERTS, dtype=jnp.int32)[None, :]).astype(jnp.int32)
    earlier = jnp.cumsum(onehot, axis=0) - onehot
    return (flat_ids * CAP + jnp.sum(earlier * onehot, axis=1)).astype(jnp.int32)


def reference(tokens, out_grad, gates, expert_ids, w_in, w_out):
    device_count = N_DP * N_EXPERT
    targets = jax.vmap(slot_positions)(expert_ids.reshape(device_count, TOK_DEV, 2))
    assignment = jnp.arange(2 * TOKEN_TOTAL, dtype=jnp.int32).reshape(device_count, 2 * TOK_DEV)
    device_rows = jnp.broadcast_to(jnp.arange(device_count, dtype=jnp.int32)[:, None], targets.shape)
    slot_table = jnp.full((device_count, EXPERTS * CAP), -1, jnp.int32).at[device_rows, targets].set(assignment)
    slot_table = slot_table.reshape(N_DP, N_EXPERT, EXPERTS, CAP)
    flat_gates = gates.reshape(-1)

    def one_expert(running, expert_index):
        slot_owner = lax.dynamic_index_in_dim(slot_table, expert_index, 2, False).reshape(N_DP * ROWS)
        is_filled = slot_owner >= 0
        safe_owner = jnp.maximum(slot_owner, 0).astype(jnp.int32)
        token_row = (safe_owner // 2).astype(jnp.int32)
        rows_x = jnp.where(is_filled[:, None], tokens[token_row], jnp.zeros((), jnp.bfloat16))
        rows_dy = jnp.where(is_filled[:, None], out_grad[token_row], jnp.zeros((), jnp.bfloat16))
        gate_column = jnp.where(is_filled, flat_gates[safe_owner].astype(jnp.float32), jnp.float32(0.0))[:, None]
        w_first = lax.dynamic_index_in_dim(w_in, expert_index, 0, False)
        w_second = lax.dynamic_index_in_dim(w_out, expert_index, 0, False)
        pre_act = jnp.dot(rows_x, w_first, preferred_element_type=jnp.float32)
        activated = gelu_value(pre_act).astype(jnp.bfloat16)
        dy_proj = jnp.dot(rows_dy, w_second, preferred_element_type=jnp.float32)
        d_pre = (gate_column * dy_proj * gelu_slope(pre_act)).astype(jnp.bfloat16)
        scaled = (gate_column * activated.astype(jnp.float32)).astype(jnp.bfloat16)
        dx_rows = jnp.dot(d_pre, w_first.T, preferred_element_type=jnp.float32).astype(jnp.bfloat16)
        expert_out = jnp.dot(activated, w_second.T, preferred_element_type=jnp.float32)
        gate_rows = jnp.sum(rows_dy.astype(jnp.float32) * expert_out, axis=1).astype(jnp.bfloat16)
        input_halves = rows_x.reshape(N_DP, ROWS, D).astype(jnp.float32)
        output_gradient_halves = rows_dy.reshape(N_DP, ROWS, D).astype(jnp.float32)
        preact_gradient_halves = d_pre.reshape(N_DP, ROWS, FF).astype(jnp.float32)
        scaled_halves = scaled.reshape(N_DP, ROWS, FF).astype(jnp.float32)
        leading_portion = jnp.einsum("mcu,mcs->mus", input_halves, preact_gradient_halves)
        leading_portion = lax.optimization_barrier(leading_portion.astype(jnp.bfloat16)).astype(jnp.float32)
        trailing_portion = jnp.einsum("mcu,mcs->mus", output_gradient_halves, scaled_halves)
        trailing_portion = lax.optimization_barrier(trailing_portion.astype(jnp.bfloat16)).astype(jnp.float32)
        grad_first = jnp.sum(leading_portion, axis=0)
        grad_second = jnp.sum(trailing_portion, axis=0)
        dx_total, dg_total = running
        dx_total = dx_total.at[token_row].add(jnp.where(is_filled[:, None], dx_rows.astype(jnp.float32), jnp.float32(0.0)))
        dg_total = dg_total.at[safe_owner].add(jnp.where(is_filled, gate_rows.astype(jnp.float32), jnp.float32(0.0)))
        return (dx_total, dg_total), (grad_first, grad_second)

    initial = (jnp.zeros((TOKEN_TOTAL, D), jnp.float32), jnp.zeros((2 * TOKEN_TOTAL,), jnp.float32))
    finals, stacked = lax.scan(one_expert, initial, jnp.arange(EXPERTS, dtype=jnp.int32))
    d_tokens = finals[0].astype(jnp.bfloat16)
    gate_grad = finals[1].reshape(TOKEN_TOTAL, 2).astype(jnp.bfloat16)
    return (d_tokens, gate_grad, stacked[0], stacked[1])
```

```python
import jax
import jax.numpy as jnp
from jax import lax
from jax.experimental import pallas as pl
from jax.experimental.pallas import tpu as pltpu
from jax.sharding import PartitionSpec as P

gelu_scale = 0.7978845608028654
cubic_coef = 0.044715
bf16 = jnp.bfloat16
f32 = jnp.float32
LANES = 128
VMEM_BYTES = 56 << 20


def call(body, out_shape, name, scratch=()):
    return pl.pallas_call(
        body,
        out_shape=out_shape,
        scratch_shapes=scratch,
        name=name,
        compiler_params=pltpu.CompilerParams(vmem_limit_bytes=VMEM_BYTES),
    )


def slot_targets(ids_ref, experts, capacity):
    tokens = ids_ref.shape[1]
    first = ids_ref[0:1, :]
    second = ids_ref[1:2, :]
    expert = lax.broadcasted_iota(jnp.int32, (experts, tokens), 0)
    is_first = (expert == first).astype(f32)
    is_second = (expert == second).astype(f32)
    before = (
        lax.broadcasted_iota(jnp.int32, (tokens, tokens), 0)
        < lax.broadcasted_iota(jnp.int32, (tokens, tokens), 1)
    ).astype(f32)
    earlier = jnp.dot(
        (is_first + is_second).astype(bf16), before.astype(bf16), preferred_element_type=f32
    )
    slot_first = jnp.sum(earlier * is_first, axis=0, keepdims=True).astype(jnp.int32)
    slot_second = jnp.sum(earlier * is_second, axis=0, keepdims=True).astype(jnp.int32)
    return first * capacity + slot_first, second * capacity + slot_second


def one_hots(ids_ref, experts, capacity):
    tokens = ids_ref.shape[1]
    first, second = slot_targets(ids_ref, experts, capacity)
    slot = lax.broadcasted_iota(jnp.int32, (experts * capacity, tokens), 0)
    return (slot == first).astype(f32), (slot == second).astype(f32)


def dispatch_body(experts, capacity, ids_ref, gates_ref, x_ref, dy_ref, out_ref, wide_ref):
    width = x_ref.shape[1] // LANES
    slots = experts * capacity
    pick_first, pick_second = one_hots(ids_ref, experts, capacity)
    gates = gates_ref[...].astype(f32)
    pick = (pick_first + pick_second).astype(bf16)
    gated = (pick_first * gates[0:1, :] + pick_second * gates[1:2, :]).astype(bf16)
    rows_x = jnp.dot(pick, x_ref[...], preferred_element_type=f32)
    rows_dy = jnp.dot(gated, dy_ref[...], preferred_element_type=f32)
    for j in range(width):
        cols = slice(j * LANES, (j + 1) * LANES)
        wide_ref[pl.ds(j, slots, stride=2 * width), :] = rows_x[:, cols]
        wide_ref[pl.ds(width + j, slots, stride=2 * width), :] = rows_dy[:, cols]
    out_ref[...] = wide_ref[...].astype(bf16)


def gelu_parts(pre):
    inner = jnp.tanh(gelu_scale * (pre + cubic_coef * pre * pre * pre))
    value = 0.5 * pre * (1.0 + inner)
    slope = 0.5 * (1.0 + inner) + 0.5 * pre * (1.0 - inner * inner) * gelu_scale * (
        1.0 + 3.0 * cubic_coef * pre * pre
    )
    return value, slope


def units(x, dy, w_first, w_second):
    pre = jnp.dot(x, w_first, preferred_element_type=f32)
    dy_proj = jnp.dot(dy, w_second, preferred_element_type=f32)
    value, slope = gelu_parts(pre)
    activated = value.astype(bf16)
    d_pre = (dy_proj * slope).astype(bf16)
    gate = activated.astype(f32) * dy_proj
    grad_first = lax.dot_general(
        d_pre, x, (((0,), (0,)), ((), ())), preferred_element_type=f32
    )
    grad_second = lax.dot_general(
        activated, dy, (((0,), (0,)), ((), ())), preferred_element_type=f32
    )
    return d_pre, gate, grad_first, grad_second


def own_body(
    mine_ref, other_ref, wi_ref, wo_ref, x_ref, dy_ref, dpre_ref, gate_ref, gi_ref, go_ref, wide_ref
):
    slots = x_ref.shape[0] // 2
    width = x_ref.shape[1] // LANES
    for half, ref in enumerate((mine_ref, other_ref)):
        wide_ref[...] = ref[...].astype(f32)
        rows = slice(half * slots, (half + 1) * slots)
        for j in range(width):
            cols = slice(j * LANES, (j + 1) * LANES)
            x_ref[rows, cols] = wide_ref[pl.ds(j, slots, stride=2 * width), :].astype(bf16)
            dy_ref[rows, cols] = wide_ref[pl.ds(width + j, slots, stride=2 * width), :].astype(bf16)
    d_pre, gate, grad_first, grad_second = units(x_ref[...], dy_ref[...], wi_ref[...], wo_ref[...])
    dpre_ref[...] = d_pre
    gate_ref[...] = gate
    gi_ref[...] = grad_first
    go_ref[...] = grad_second


def near_body(
    x_ref, dy_ref, wim_ref, wom_ref, wip_ref, wop_ref, gate_in_ref,
    dpre_ref, gate_ref, gim_ref, gom_ref, gip_ref, gop_ref,
):
    w_first = jnp.concatenate([wim_ref[...], wip_ref[...]], axis=1)
    w_second = jnp.concatenate([wom_ref[...], wop_ref[...]], axis=1)
    d_pre, gate, grad_first, grad_second = units(x_ref[...], dy_ref[...], w_first, w_second)
    dpre_ref[...] = d_pre
    gate_ref[...] = gate_in_ref[...] + gate[:, :LANES] + gate[:, LANES:]
    gim_ref[...] = grad_first[:LANES].astype(bf16)
    gip_ref[...] = grad_first[LANES:].astype(bf16)
    gom_ref[...] = grad_second[:LANES].astype(bf16)
    gop_ref[...] = grad_second[LANES:].astype(bf16)


def far_body(x_ref, dy_ref, wi_ref, wo_ref, gate_in_ref, dpre_ref, gate_ref, gi_ref, go_ref):
    d_pre, gate, grad_first, grad_second = units(x_ref[...], dy_ref[...], wi_ref[...], wo_ref[...])
    dpre_ref[...] = d_pre
    gate_ref[...] = gate_in_ref[...] + gate
    gi_ref[...] = grad_first.astype(bf16)
    go_ref[...] = grad_second.astype(bf16)


def dx_body(
    dpre0_ref, dpre1_ref, dpre2_ref, w0_ref, wm_ref, wp_ref, wf_ref, gate_ref,
    keep_ref, keep_gate_ref, give_ref,
):
    slots = keep_ref.shape[0]
    width = keep_ref.shape[1]
    d_pre = jnp.concatenate([dpre0_ref[...], dpre1_ref[...], dpre2_ref[...]], axis=1)
    weights = jnp.concatenate([w0_ref[...], wm_ref[...], wp_ref[...], wf_ref[...]], axis=1)
    dx = lax.dot_general(d_pre, weights, (((1,), (1,)), ((), ())), preferred_element_type=f32)
    gate = jnp.sum(gate_ref[...], axis=1, keepdims=True)
    keep_ref[...] = dx[:slots]
    keep_gate_ref[...] = jnp.broadcast_to(gate[:slots], keep_gate_ref.shape)
    give_ref[:, :width] = dx[slots:].astype(bf16)
    coarse = gate[slots:].astype(bf16)
    fine = (gate[slots:] - coarse.astype(f32)).astype(bf16)
    lane = lax.broadcasted_iota(jnp.int32, (slots, LANES), 1)
    give_ref[:, width:] = jnp.where(
        lane == 0, coarse.astype(f32), jnp.where(lane == 1, fine.astype(f32), 0.0)
    ).astype(bf16)


def pack_body(experts, capacity, keep_ref, keep_gate_ref, took_ref, out_ref, rows_ref, wide_ref):
    slots = keep_ref.shape[0]
    width = keep_ref.shape[1]
    tiles = width // LANES
    step = (capacity + 1) * tiles
    for j in range(tiles):
        cols = slice(j * LANES, (j + 1) * LANES)
        total = keep_ref[:, cols] + took_ref[:, cols].astype(f32)
        rows_ref[j] = total.astype(bf16).astype(f32)
    gate = keep_gate_ref[:, 0:1] + jnp.sum(took_ref[:, width:].astype(f32), axis=1, keepdims=True)
    row = lax.broadcasted_iota(jnp.int32, (slots, LANES), 0)
    lane = lax.broadcasted_iota(jnp.int32, (slots, LANES), 1)
    spread = jnp.where(row % capacity == lane, gate, 0.0).astype(bf16)
    expert = lax.broadcasted_iota(jnp.int32, (experts, slots), 0)
    slot = lax.broadcasted_iota(jnp.int32, (experts, slots), 1)
    owner = (slot // capacity == expert).astype(f32).astype(bf16)
    table = jnp.dot(owner, spread, preferred_element_type=f32)
    for c in range(capacity):
        for j in range(tiles):
            wide_ref[pl.ds(c * tiles + j, experts, stride=step), :] = rows_ref[
                j, pl.ds(c, experts, stride=capacity), :
            ]
    for j in range(tiles):
        wide_ref[pl.ds(capacity * tiles + j, experts, stride=step), :] = (
            table if j == 0 else jnp.zeros_like(table)
        )
    out_ref[...] = wide_ref[...].astype(bf16)


def combine_body(
    experts, capacity, ids_ref, gates_ref, back_ref, dtok_ref, dgate_ref, wide_ref, rows_ref
):
    slots = experts * capacity
    tiles = dtok_ref.shape[1] // LANES
    step = (capacity + 1) * tiles
    wide_ref[...] = back_ref[...].astype(f32)
    for c in range(capacity):
        for j in range(tiles):
            rows_ref[j, pl.ds(c, experts, stride=capacity), :] = wide_ref[
                pl.ds(c * tiles + j, experts, stride=step), :
            ]
    table = wide_ref[pl.ds(capacity * tiles, experts, stride=step), :].astype(bf16)
    pick_first, pick_second = one_hots(ids_ref, experts, capacity)
    pick = (pick_first + pick_second).astype(bf16)
    for j in range(tiles):
        dtok_ref[:, j * LANES : (j + 1) * LANES] = lax.dot_general(
            pick, rows_ref[j].astype(bf16), (((0,), (0,)), ((), ())), preferred_element_type=f32
        ).astype(bf16)
    expert = lax.broadcasted_iota(jnp.int32, (slots, experts), 1)
    slot = lax.broadcasted_iota(jnp.int32, (slots, experts), 0)
    owner = (slot // capacity == expert).astype(f32).astype(bf16)
    by_slot = jnp.dot(owner, table, preferred_element_type=f32)
    row = lax.broadcasted_iota(jnp.int32, (slots, LANES), 0)
    lane = lax.broadcasted_iota(jnp.int32, (slots, LANES), 1)
    gate = jnp.sum(jnp.where(row % capacity == lane, by_slot, 0.0), axis=1, keepdims=True)
    gates = gates_ref[...].astype(f32)
    sums = jnp.concatenate(
        [
            jnp.sum(pick_first * gate, axis=0, keepdims=True),
            jnp.sum(pick_second * gate, axis=0, keepdims=True),
        ],
        axis=0,
    )
    dgate_ref[...] = (sums / gates).astype(bf16)


def add_body(a_ref, b_ref, c_ref, d_ref, first_ref, second_ref):
    first_ref[...] = (a_ref[...].astype(f32) + b_ref[...].astype(f32)).astype(bf16)
    second_ref[...] = (c_ref[...].astype(f32) + d_ref[...].astype(f32)).astype(bf16)


def finish_body(own_i, a_i, c_i, own_o, a_o, c_o, gi_ref, go_ref):
    gi_ref[...] = (own_i[...] + a_i[...].astype(f32) + c_i[...].astype(f32)).T
    go_ref[...] = (own_o[...] + a_o[...].astype(f32) + c_o[...].astype(f32)).T


def shards(tokens, out_grad, gates, expert_ids, w_in, w_out):
    tok_rows, width = tokens.shape
    experts = lax.axis_size("expert")
    replicas = lax.axis_size("dp")
    capacity = 3 * tok_rows // experts
    slots = experts * capacity
    tiles = width // LANES
    shard = w_in.shape[2]
    up = [(i, (i + 2) % replicas) for i in range(replicas)]
    down = [(i, (i - 2) % replicas) for i in range(replicas)]
    swap = [(i, i ^ 1) for i in range(replicas)]
    sds = jax.ShapeDtypeStruct

    def send(value, perm):
        return lax.ppermute(value, "dp", perm)

    wi = w_in.reshape(width, shard)
    wo = w_out.reshape(width, shard)
    ids = expert_ids.T
    gates_row = gates.T

    wi_m = send(wi, up)
    wo_p = send(wo, down)
    wi_p = send(wi, down)
    wo_m = send(wo, up)
    wi_f = send(wi_m, up)
    wo_f = send(wo_p, down)

    payload = call(
        lambda *refs: dispatch_body(experts, capacity, *refs),
        sds((slots * 2 * tiles, LANES), bf16),
        "dispatch",
        [pltpu.VMEM((slots * 2 * tiles, LANES), f32)],
    )(ids, gates_row, tokens, out_grad)
    mine = lax.all_to_all(
        payload.reshape(experts, capacity * 2 * tiles, LANES),
        "expert", split_axis=0, concat_axis=0, tiled=True,
    ).reshape(slots * 2 * tiles, LANES)
    other = send(mine, swap)

    rows = sds((2 * slots, width), bf16)
    gate_shape = sds((2 * slots, LANES), f32)
    grad = sds((shard, width), bf16)
    x, dy, dpre0, gate0, own_i, own_o = call(
        own_body,
        (rows, rows, sds((2 * slots, shard), bf16), gate_shape,
         sds((shard, width), f32), sds((shard, width), f32)),
        "own_units",
        [pltpu.VMEM((slots * 2 * tiles, LANES), f32)],
    )(mine, other, wi, wo)
    dpre1, gate1, gi_m, go_m, gi_p, go_p = call(
        near_body,
        (sds((2 * slots, 2 * shard), bf16), gate_shape, grad, grad, grad, grad),
        "near_units",
    )(x, dy, wi_m, wo_m, wi_p, wo_p, gate0)
    a_o = send(go_p, up)
    a_i = send(gi_m, down)
    dpre2, gate2, gi_f, go_f = call(
        far_body,
        (sds((2 * slots, shard), bf16), gate_shape, grad, grad),
        "far_units",
    )(x, dy, wi_f, wo_f, gate1)
    b_i = send(gi_f, up)
    b_o = send(go_f, down)
    keep, keep_gate, give = call(
        dx_body,
        (sds((slots, width), f32), sds((slots, LANES), f32), sds((slots, width + LANES), bf16)),
        "input_gradient",
    )(dpre0, dpre1, dpre2, wi, wi_m, wi_p, wi_f, gate2)
    took = send(give, swap)
    back = call(
        lambda *refs: pack_body(experts, capacity, *refs),
        sds((experts * (capacity + 1) * tiles, LANES), bf16),
        "pack",
        [
            pltpu.VMEM((tiles, slots, LANES), f32),
            pltpu.VMEM((experts * (capacity + 1) * tiles, LANES), f32),
        ],
    )(keep, keep_gate, took)
    back = lax.all_to_all(
        back.reshape(experts, (capacity + 1) * tiles, LANES),
        "expert", split_axis=0, concat_axis=0, tiled=True,
    ).reshape(experts * (capacity + 1) * tiles, LANES)
    sum_i, sum_o = call(add_body, (grad, grad), "add_far")(gi_p, b_i, go_m, b_o)
    c_i = send(sum_i, up)
    c_o = send(sum_o, down)
    d_tokens, gate_grad = call(
        lambda *refs: combine_body(experts, capacity, *refs),
        (sds((tok_rows, width), bf16), sds((2, tok_rows), bf16)),
        "combine",
        [
            pltpu.VMEM((experts * (capacity + 1) * tiles, LANES), f32),
            pltpu.VMEM((tiles, slots, LANES), f32),
        ],
    )(ids, gates_row, back)
    total = sds((width, shard), f32)
    grad_in, grad_out = call(finish_body, (total, total), "finish")(
        own_i, a_i, c_i, own_o, a_o, c_o
    )
    return d_tokens, gate_grad.T, grad_in[None], grad_out[None]


def solution(mesh):
    by_token = P(("dp", "expert"), None)
    by_expert = P("expert", None, "dp")
    return jax.shard_map(
        shards,
        mesh=mesh,
        in_specs=(by_token, by_token, by_token, by_token, by_expert, by_expert),
        out_specs=(by_token, by_token, by_expert, by_expert),
        check_vma=False,
    )
```

```python
import jax
import jax.numpy as jnp
from jax import lax
from jax.experimental import pallas as pl
from jax.experimental.pallas import tpu as pltpu
from jax.sharding import PartitionSpec as P

gelu_scale = 0.7978845608028654
cubic_coef = 0.044715
bf16 = jnp.bfloat16
f32 = jnp.float32
LANES = 128
VMEM_BYTES = 56 << 20


def call(body, out_shape, name, scratch=()):
    return pl.pallas_call(
        body,
        out_shape=out_shape,
        scratch_shapes=scratch,
        name=name,
        compiler_params=pltpu.CompilerParams(vmem_limit_bytes=VMEM_BYTES),
    )


def slot_targets(ids_ref, experts, capacity):
    tokens = ids_ref.shape[1]
    first = ids_ref[0:1, :]
    second = ids_ref[1:2, :]
    expert = lax.broadcasted_iota(jnp.int32, (experts, tokens), 0)
    is_first = (expert == first).astype(f32)
    is_second = (expert == second).astype(f32)
    before = (
        lax.broadcasted_iota(jnp.int32, (tokens, tokens), 0)
        < lax.broadcasted_iota(jnp.int32, (tokens, tokens), 1)
    ).astype(f32)
    earlier = jnp.dot(
        (is_first + is_second).astype(bf16), before.astype(bf16), preferred_element_type=f32
    )
    slot_first = jnp.sum(earlier * is_first, axis=0, keepdims=True).astype(jnp.int32)
    slot_second = jnp.sum(earlier * is_second, axis=0, keepdims=True).astype(jnp.int32)
    return first * capacity + slot_first, second * capacity + slot_second


def one_hots(ids_ref, experts, capacity):
    tokens = ids_ref.shape[1]
    first, second = slot_targets(ids_ref, experts, capacity)
    slot = lax.broadcasted_iota(jnp.int32, (experts * capacity, tokens), 0)
    return (slot == first).astype(f32), (slot == second).astype(f32)


def dispatch_body(experts, capacity, ids_ref, gates_ref, x_ref, dy_ref, out_ref, wide_ref):
    width = x_ref.shape[1] // LANES
    slots = experts * capacity
    pick_first, pick_second = one_hots(ids_ref, experts, capacity)
    gates = gates_ref[...].astype(f32)
    pick = (pick_first + pick_second).astype(bf16)
    gated = (pick_first * gates[0:1, :] + pick_second * gates[1:2, :]).astype(bf16)
    rows_x = jnp.dot(pick, x_ref[...], preferred_element_type=f32)
    rows_dy = jnp.dot(gated, dy_ref[...], preferred_element_type=f32)
    for j in range(width):
        cols = slice(j * LANES, (j + 1) * LANES)
        wide_ref[pl.ds(j, slots, stride=2 * width), :] = rows_x[:, cols]
        wide_ref[pl.ds(width + j, slots, stride=2 * width), :] = rows_dy[:, cols]
    out_ref[...] = wide_ref[...].astype(bf16)


def gelu_parts(pre):
    inner = jnp.tanh(gelu_scale * (pre + cubic_coef * pre * pre * pre))
    value = 0.5 * pre * (1.0 + inner)
    slope = 0.5 * (1.0 + inner) + 0.5 * pre * (1.0 - inner * inner) * gelu_scale * (
        1.0 + 3.0 * cubic_coef * pre * pre
    )
    return value, slope


def units(x, dy, w_first, w_second):
    pre = jnp.dot(x, w_first, preferred_element_type=f32)
    dy_proj = jnp.dot(dy, w_second, preferred_element_type=f32)
    value, slope = gelu_parts(pre)
    activated = value.astype(bf16)
    d_pre = (dy_proj * slope).astype(bf16)
    gate = activated.astype(f32) * dy_proj
    grad_first = lax.dot_general(
        d_pre, x, (((0,), (0,)), ((), ())), preferred_element_type=f32
    )
    grad_second = lax.dot_general(
        activated, dy, (((0,), (0,)), ((), ())), preferred_element_type=f32
    )
    return d_pre, gate, grad_first, grad_second


def own_body(
    mine_ref, other_ref, wi_ref, wo_ref, x_ref, dy_ref, dpre_ref, gate_ref, gi_ref, go_ref, wide_ref
):
    slots = x_ref.shape[0] // 2
    width = x_ref.shape[1] // LANES
    for half, ref in enumerate((mine_ref, other_ref)):
        wide_ref[...] = ref[...].astype(f32)
        rows = slice(half * slots, (half + 1) * slots)
        for j in range(width):
            cols = slice(j * LANES, (j + 1) * LANES)
            x_ref[rows, cols] = wide_ref[pl.ds(j, slots, stride=2 * width), :].astype(bf16)
            dy_ref[rows, cols] = wide_ref[pl.ds(width + j, slots, stride=2 * width), :].astype(bf16)
    d_pre, gate, grad_first, grad_second = units(x_ref[...], dy_ref[...], wi_ref[...], wo_ref[...])
    dpre_ref[...] = d_pre
    gate_ref[...] = gate
    gi_ref[...] = grad_first
    go_ref[...] = grad_second


def near_body(
    x_ref, dy_ref, wm_ref, wp_ref, gate_in_ref,
    dpre_ref, gate_ref, gim_ref, gom_ref, gip_ref, gop_ref,
):
    width = x_ref.shape[1]
    w_first = jnp.concatenate([wm_ref[:width], wp_ref[:width]], axis=1)
    w_second = jnp.concatenate([wm_ref[width:], wp_ref[width:]], axis=1)
    d_pre, gate, grad_first, grad_second = units(x_ref[...], dy_ref[...], w_first, w_second)
    dpre_ref[...] = d_pre
    gate_ref[...] = gate_in_ref[...] + gate[:, :LANES] + gate[:, LANES:]
    gim_ref[...] = grad_first[:LANES].astype(bf16)
    gip_ref[...] = grad_first[LANES:].astype(bf16)
    gom_ref[...] = grad_second[:LANES].astype(bf16)
    gop_ref[...] = grad_second[LANES:].astype(bf16)


def far_body(x_ref, dy_ref, wi_ref, wo_ref, gate_in_ref, dpre_ref, gate_ref, gi_ref, go_ref):
    d_pre, gate, grad_first, grad_second = units(x_ref[...], dy_ref[...], wi_ref[...], wo_ref[...])
    dpre_ref[...] = d_pre
    gate_ref[...] = gate_in_ref[...] + gate
    gi_ref[...] = grad_first.astype(bf16)
    go_ref[...] = grad_second.astype(bf16)


def dx_body(
    dpre0_ref, dpre1_ref, dpre2_ref, w0_ref, wm_ref, wp_ref, wf_ref, gate_ref,
    keep_ref, keep_gate_ref, give_ref,
):
    slots = keep_ref.shape[0]
    width = keep_ref.shape[1]
    d_pre = jnp.concatenate([dpre0_ref[...], dpre1_ref[...], dpre2_ref[...]], axis=1)
    weights = jnp.concatenate([w0_ref[...], wm_ref[:width], wp_ref[:width], wf_ref[...]], axis=1)
    dx = lax.dot_general(d_pre, weights, (((1,), (1,)), ((), ())), preferred_element_type=f32)
    gate = jnp.sum(gate_ref[...], axis=1, keepdims=True)
    keep_ref[...] = dx[:slots]
    keep_gate_ref[...] = jnp.broadcast_to(gate[:slots], keep_gate_ref.shape)
    give_ref[:, :width] = dx[slots:].astype(bf16)
    coarse = gate[slots:].astype(bf16)
    fine = (gate[slots:] - coarse.astype(f32)).astype(bf16)
    lane = lax.broadcasted_iota(jnp.int32, (slots, LANES), 1)
    give_ref[:, width:] = jnp.where(
        lane == 0, coarse.astype(f32), jnp.where(lane == 1, fine.astype(f32), 0.0)
    ).astype(bf16)


def pack_body(experts, capacity, keep_ref, keep_gate_ref, took_ref, out_ref, rows_ref, wide_ref):
    slots = keep_ref.shape[0]
    width = keep_ref.shape[1]
    tiles = width // LANES
    step = (capacity + 1) * tiles
    for j in range(tiles):
        cols = slice(j * LANES, (j + 1) * LANES)
        total = keep_ref[:, cols] + took_ref[:, cols].astype(f32)
        rows_ref[j] = total.astype(bf16).astype(f32)
    gate = keep_gate_ref[:, 0:1] + jnp.sum(took_ref[:, width:].astype(f32), axis=1, keepdims=True)
    row = lax.broadcasted_iota(jnp.int32, (slots, LANES), 0)
    lane = lax.broadcasted_iota(jnp.int32, (slots, LANES), 1)
    spread = jnp.where(row % capacity == lane, gate, 0.0).astype(bf16)
    expert = lax.broadcasted_iota(jnp.int32, (experts, slots), 0)
    slot = lax.broadcasted_iota(jnp.int32, (experts, slots), 1)
    owner = (slot // capacity == expert).astype(f32).astype(bf16)
    table = jnp.dot(owner, spread, preferred_element_type=f32)
    for c in range(capacity):
        for j in range(tiles):
            wide_ref[pl.ds(c * tiles + j, experts, stride=step), :] = rows_ref[
                j, pl.ds(c, experts, stride=capacity), :
            ]
    for j in range(tiles):
        wide_ref[pl.ds(capacity * tiles + j, experts, stride=step), :] = (
            table if j == 0 else jnp.zeros_like(table)
        )
    out_ref[...] = wide_ref[...].astype(bf16)


def combine_body(
    experts, capacity, ids_ref, gates_ref, back_ref, dtok_ref, dgate_ref, wide_ref, rows_ref
):
    slots = experts * capacity
    tiles = dtok_ref.shape[1] // LANES
    step = (capacity + 1) * tiles
    wide_ref[...] = back_ref[...].astype(f32)
    for c in range(capacity):
        for j in range(tiles):
            rows_ref[j, pl.ds(c, experts, stride=capacity), :] = wide_ref[
                pl.ds(c * tiles + j, experts, stride=step), :
            ]
    table = wide_ref[pl.ds(capacity * tiles, experts, stride=step), :].astype(bf16)
    pick_first, pick_second = one_hots(ids_ref, experts, capacity)
    pick = (pick_first + pick_second).astype(bf16)
    for j in range(tiles):
        dtok_ref[:, j * LANES : (j + 1) * LANES] = lax.dot_general(
            pick, rows_ref[j].astype(bf16), (((0,), (0,)), ((), ())), preferred_element_type=f32
        ).astype(bf16)
    expert = lax.broadcasted_iota(jnp.int32, (slots, experts), 1)
    slot = lax.broadcasted_iota(jnp.int32, (slots, experts), 0)
    owner = (slot // capacity == expert).astype(f32).astype(bf16)
    by_slot = jnp.dot(owner, table, preferred_element_type=f32)
    row = lax.broadcasted_iota(jnp.int32, (slots, LANES), 0)
    lane = lax.broadcasted_iota(jnp.int32, (slots, LANES), 1)
    gate = jnp.sum(jnp.where(row % capacity == lane, by_slot, 0.0), axis=1, keepdims=True)
    gates = gates_ref[...].astype(f32)
    sums = jnp.concatenate(
        [
            jnp.sum(pick_first * gate, axis=0, keepdims=True),
            jnp.sum(pick_second * gate, axis=0, keepdims=True),
        ],
        axis=0,
    )
    dgate_ref[...] = (sums / gates).astype(bf16)


def add_body(near_i, far_i, near_o, far_o, own_i, a_i, own_o, a_o, si_ref, so_ref, ti_ref, to_ref):
    si_ref[...] = (near_i[...].astype(f32) + far_i[...].astype(f32)).astype(bf16)
    so_ref[...] = (near_o[...].astype(f32) + far_o[...].astype(f32)).astype(bf16)
    ti_ref[...] = own_i[...] + a_i[...].astype(f32)
    to_ref[...] = own_o[...] + a_o[...].astype(f32)


def finish_body(total_i, c_i, total_o, c_o, gi_ref, go_ref):
    gi_ref[...] = (total_i[...] + c_i[...].astype(f32)).T
    go_ref[...] = (total_o[...] + c_o[...].astype(f32)).T


def shards(tokens, out_grad, gates, expert_ids, w_in, w_out):
    tok_rows, width = tokens.shape
    experts = lax.axis_size("expert")
    replicas = lax.axis_size("dp")
    capacity = 3 * tok_rows // experts
    slots = experts * capacity
    tiles = width // LANES
    shard = w_in.shape[2]
    up = [(i, (i + 2) % replicas) for i in range(replicas)]
    down = [(i, (i - 2) % replicas) for i in range(replicas)]
    swap = [(i, i ^ 1) for i in range(replicas)]
    sds = jax.ShapeDtypeStruct

    def send(value, perm):
        return lax.ppermute(value, "dp", perm)

    wi = w_in.reshape(width, shard)
    wo = w_out.reshape(width, shard)
    ids = expert_ids.T
    gates_row = gates.T

    both = jnp.concatenate([wi, wo], axis=0)
    w_m = send(both, up)
    w_p = send(both, down)

    payload = call(
        lambda *refs: dispatch_body(experts, capacity, *refs),
        sds((slots * 2 * tiles, LANES), bf16),
        "dispatch",
        [pltpu.VMEM((slots * 2 * tiles, LANES), f32)],
    )(ids, gates_row, tokens, out_grad)
    mine = lax.all_to_all(
        payload.reshape(experts, capacity * 2 * tiles, LANES),
        "expert", split_axis=0, concat_axis=0, tiled=True,
    ).reshape(slots * 2 * tiles, LANES)
    wi_f = send(w_m[:width], up)
    wo_f = send(w_p[width:], down)
    mine, w_m, w_p = lax.optimization_barrier((mine, w_m, w_p))
    other = send(mine, swap)

    rows = sds((2 * slots, width), bf16)
    gate_shape = sds((2 * slots, LANES), f32)
    grad = sds((shard, width), bf16)
    x, dy, dpre0, gate0, own_i, own_o = call(
        own_body,
        (rows, rows, sds((2 * slots, shard), bf16), gate_shape,
         sds((shard, width), f32), sds((shard, width), f32)),
        "own_units",
        [pltpu.VMEM((slots * 2 * tiles, LANES), f32)],
    )(mine, other, wi, wo)
    dpre1, gate1, gi_m, go_m, gi_p, go_p = call(
        near_body,
        (sds((2 * slots, 2 * shard), bf16), gate_shape, grad, grad, grad, grad),
        "near_units",
    )(x, dy, w_m, w_p, gate0)
    a_o = send(go_p, up)
    a_i = send(gi_m, down)
    dpre2, gate2, gi_f, go_f = call(
        far_body,
        (sds((2 * slots, shard), bf16), gate_shape, grad, grad),
        "far_units",
    )(x, dy, wi_f, wo_f, gate1)
    b_i = send(gi_f, up)
    b_o = send(go_f, down)
    gate2, a_i, a_o = lax.optimization_barrier((gate2, a_i, a_o))
    keep, keep_gate, give = call(
        dx_body,
        (sds((slots, width), f32), sds((slots, LANES), f32), sds((slots, width + LANES), bf16)),
        "input_gradient",
    )(dpre0, dpre1, dpre2, wi, w_m, w_p, wi_f, gate2)
    took = send(give, swap)
    back = call(
        lambda *refs: pack_body(experts, capacity, *refs),
        sds((experts * (capacity + 1) * tiles, LANES), bf16),
        "pack",
        [
            pltpu.VMEM((tiles, slots, LANES), f32),
            pltpu.VMEM((experts * (capacity + 1) * tiles, LANES), f32),
        ],
    )(keep, keep_gate, took)
    part = sds((shard, width), f32)
    sum_i, sum_o, part_i, part_o = call(add_body, (grad, grad, part, part), "add_far")(
        gi_p, b_i, go_m, b_o, own_i, a_i, own_o, a_o
    )
    back, sum_i, sum_o = lax.optimization_barrier((back, sum_i, sum_o))
    back = lax.all_to_all(
        back.reshape(experts, (capacity + 1) * tiles, LANES),
        "expert", split_axis=0, concat_axis=0, tiled=True,
    ).reshape(experts * (capacity + 1) * tiles, LANES)
    c_i = send(sum_i, up)
    c_o = send(sum_o, down)
    d_tokens, gate_grad = call(
        lambda *refs: combine_body(experts, capacity, *refs),
        (sds((tok_rows, width), bf16), sds((2, tok_rows), bf16)),
        "combine",
        [
            pltpu.VMEM((experts * (capacity + 1) * tiles, LANES), f32),
            pltpu.VMEM((tiles, slots, LANES), f32),
        ],
    )(ids, gates_row, back)
    total = sds((width, shard), f32)
    grad_in, grad_out = call(finish_body, (total, total), "finish")(
        part_i, c_i, part_o, c_o
    )
    return d_tokens, gate_grad.T, grad_in[None], grad_out[None]


def solution(mesh):
    by_token = P(("dp", "expert"), None)
    by_expert = P("expert", None, "dp")
    return jax.shard_map(
        shards,
        mesh=mesh,
        in_specs=(by_token, by_token, by_token, by_token, by_expert, by_expert),
        out_specs=(by_token, by_token, by_expert, by_expert),
        check_vma=False,
    )
```

```python
import jax
import jax.numpy as jnp
from jax import lax
from jax.experimental import pallas as pl
from jax.experimental.pallas import tpu as pltpu
from jax.sharding import PartitionSpec as P

gelu_scale = 0.7978845608028654
cubic_coef = 0.044715
bf16 = jnp.bfloat16
f32 = jnp.float32
LANES = 128
VMEM_BYTES = 56 << 20


def call(body, out_shape, name, scratch=()):
    return pl.pallas_call(
        body,
        out_shape=out_shape,
        scratch_shapes=scratch,
        name=name,
        compiler_params=pltpu.CompilerParams(vmem_limit_bytes=VMEM_BYTES),
    )


def slot_targets(ids_ref, experts, capacity):
    tokens = ids_ref.shape[1]
    first = ids_ref[0:1, :]
    second = ids_ref[1:2, :]
    expert = lax.broadcasted_iota(jnp.int32, (experts, tokens), 0)
    is_first = (expert == first).astype(f32)
    is_second = (expert == second).astype(f32)
    before = (
        lax.broadcasted_iota(jnp.int32, (tokens, tokens), 0)
        < lax.broadcasted_iota(jnp.int32, (tokens, tokens), 1)
    ).astype(f32)
    earlier = jnp.dot(
        (is_first + is_second).astype(bf16), before.astype(bf16), preferred_element_type=f32
    )
    slot_first = jnp.sum(earlier * is_first, axis=0, keepdims=True).astype(jnp.int32)
    slot_second = jnp.sum(earlier * is_second, axis=0, keepdims=True).astype(jnp.int32)
    return first * capacity + slot_first, second * capacity + slot_second


def one_hots(ids_ref, experts, capacity):
    tokens = ids_ref.shape[1]
    first, second = slot_targets(ids_ref, experts, capacity)
    slot = lax.broadcasted_iota(jnp.int32, (experts * capacity, tokens), 0)
    return (slot == first).astype(f32), (slot == second).astype(f32)


def dispatch_body(experts, capacity, ids_ref, gates_ref, x_ref, dy_ref, out_ref, wide_ref):
    width = x_ref.shape[1] // LANES
    slots = experts * capacity
    pick_first, pick_second = one_hots(ids_ref, experts, capacity)
    gates = gates_ref[...].astype(f32)
    pick = (pick_first + pick_second).astype(bf16)
    gated = (pick_first * gates[0:1, :] + pick_second * gates[1:2, :]).astype(bf16)
    rows_x = jnp.dot(pick, x_ref[...], preferred_element_type=f32)
    rows_dy = jnp.dot(gated, dy_ref[...], preferred_element_type=f32)
    for j in range(width):
        cols = slice(j * LANES, (j + 1) * LANES)
        wide_ref[pl.ds(j, slots, stride=2 * width), :] = rows_x[:, cols]
        wide_ref[pl.ds(width + j, slots, stride=2 * width), :] = rows_dy[:, cols]
    out_ref[...] = wide_ref[...].astype(bf16)


def gelu_parts(pre):
    inner = jnp.tanh(gelu_scale * (pre + cubic_coef * pre * pre * pre))
    value = 0.5 * pre * (1.0 + inner)
    slope = 0.5 * (1.0 + inner) + 0.5 * pre * (1.0 - inner * inner) * gelu_scale * (
        1.0 + 3.0 * cubic_coef * pre * pre
    )
    return value, slope


def unpack_body(mine_ref, other_ref, x_ref, dy_ref, wide_ref):
    slots = x_ref.shape[0] // 2
    width = x_ref.shape[1] // LANES
    for half, ref in enumerate((mine_ref, other_ref)):
        wide_ref[...] = ref[...].astype(f32)
        rows = slice(half * slots, (half + 1) * slots)
        for j in range(width):
            cols = slice(j * LANES, (j + 1) * LANES)
            x_ref[rows, cols] = wide_ref[pl.ds(j, slots, stride=2 * width), :].astype(bf16)
            dy_ref[rows, cols] = wide_ref[pl.ds(width + j, slots, stride=2 * width), :].astype(bf16)


def units_body(x_ref, dy_ref, w_ref, dpre_ref, gate_ref, grad_ref):
    blocks = w_ref.shape[0]
    width = x_ref.shape[1]
    x = x_ref[...]
    dy = dy_ref[...]
    gates = []
    for pair in range(0, blocks, 2):
        w_first = jnp.concatenate([w_ref[pair, :width], w_ref[pair + 1, :width]], axis=1)
        w_second = jnp.concatenate([w_ref[pair, width:], w_ref[pair + 1, width:]], axis=1)
        pre = jnp.dot(x, w_first, preferred_element_type=f32)
        dy_proj = jnp.dot(dy, w_second, preferred_element_type=f32)
        value, slope = gelu_parts(pre)
        activated = value.astype(bf16)
        d_pre = (dy_proj * slope).astype(bf16)
        gate = activated.astype(f32) * dy_proj
        gates += [gate[:, :LANES], gate[:, LANES:]]
        dpre_ref[:, pair * LANES : (pair + 2) * LANES] = d_pre
        for row, left, right in ((0, d_pre, x), (LANES, activated, dy)):
            grad = lax.dot_general(
                left, right, (((0,), (0,)), ((), ())), preferred_element_type=f32
            ).astype(bf16)
            grad_ref[pair, row : row + LANES] = grad[:LANES]
            grad_ref[pair + 1, row : row + LANES] = grad[LANES:]
    gate_ref[...] = sum(gates[1:], gates[0])


def dx_body(dpre_ref, w_ref, gate_ref, keep_ref, keep_gate_ref, give_ref):
    slots = keep_ref.shape[0]
    width = keep_ref.shape[1]
    d_pre = dpre_ref[...]
    weights = jnp.concatenate([w_ref[i, :width] for i in range(w_ref.shape[0])], axis=1)
    dx = lax.dot_general(d_pre, weights, (((1,), (1,)), ((), ())), preferred_element_type=f32)
    gate = jnp.sum(gate_ref[...], axis=1, keepdims=True)
    keep_ref[...] = dx[:slots]
    keep_gate_ref[...] = jnp.broadcast_to(gate[:slots], keep_gate_ref.shape)
    give_ref[:, :width] = dx[slots:].astype(bf16)
    coarse = gate[slots:].astype(bf16)
    fine = (gate[slots:] - coarse.astype(f32)).astype(bf16)
    lane = lax.broadcasted_iota(jnp.int32, (slots, LANES), 1)
    give_ref[:, width:] = jnp.where(
        lane == 0, coarse.astype(f32), jnp.where(lane == 1, fine.astype(f32), 0.0)
    ).astype(bf16)


def pack_body(experts, capacity, keep_ref, keep_gate_ref, took_ref, out_ref, rows_ref, wide_ref):
    slots = keep_ref.shape[0]
    width = keep_ref.shape[1]
    tiles = width // LANES
    step = (capacity + 1) * tiles
    for j in range(tiles):
        cols = slice(j * LANES, (j + 1) * LANES)
        total = keep_ref[:, cols] + took_ref[:, cols].astype(f32)
        rows_ref[j] = total.astype(bf16).astype(f32)
    gate = keep_gate_ref[:, 0:1] + jnp.sum(took_ref[:, width:].astype(f32), axis=1, keepdims=True)
    row = lax.broadcasted_iota(jnp.int32, (slots, LANES), 0)
    lane = lax.broadcasted_iota(jnp.int32, (slots, LANES), 1)
    spread = jnp.where(row % capacity == lane, gate, 0.0).astype(bf16)
    expert = lax.broadcasted_iota(jnp.int32, (experts, slots), 0)
    slot = lax.broadcasted_iota(jnp.int32, (experts, slots), 1)
    owner = (slot // capacity == expert).astype(f32).astype(bf16)
    table = jnp.dot(owner, spread, preferred_element_type=f32)
    for c in range(capacity):
        for j in range(tiles):
            wide_ref[pl.ds(c * tiles + j, experts, stride=step), :] = rows_ref[
                j, pl.ds(c, experts, stride=capacity), :
            ]
    for j in range(tiles):
        wide_ref[pl.ds(capacity * tiles + j, experts, stride=step), :] = (
            table if j == 0 else jnp.zeros_like(table)
        )
    out_ref[...] = wide_ref[...].astype(bf16)


def combine_body(
    experts, capacity, ids_ref, gates_ref, back_ref, dtok_ref, dgate_ref, wide_ref, rows_ref
):
    slots = experts * capacity
    tiles = dtok_ref.shape[1] // LANES
    step = (capacity + 1) * tiles
    wide_ref[...] = back_ref[...].astype(f32)
    for c in range(capacity):
        for j in range(tiles):
            rows_ref[j, pl.ds(c, experts, stride=capacity), :] = wide_ref[
                pl.ds(c * tiles + j, experts, stride=step), :
            ]
    table = wide_ref[pl.ds(capacity * tiles, experts, stride=step), :].astype(bf16)
    pick_first, pick_second = one_hots(ids_ref, experts, capacity)
    pick = (pick_first + pick_second).astype(bf16)
    for j in range(tiles):
        dtok_ref[:, j * LANES : (j + 1) * LANES] = lax.dot_general(
            pick, rows_ref[j].astype(bf16), (((0,), (0,)), ((), ())), preferred_element_type=f32
        ).astype(bf16)
    expert = lax.broadcasted_iota(jnp.int32, (slots, experts), 1)
    slot = lax.broadcasted_iota(jnp.int32, (slots, experts), 0)
    owner = (slot // capacity == expert).astype(f32).astype(bf16)
    by_slot = jnp.dot(owner, table, preferred_element_type=f32)
    row = lax.broadcasted_iota(jnp.int32, (slots, LANES), 0)
    lane = lax.broadcasted_iota(jnp.int32, (slots, LANES), 1)
    gate = jnp.sum(jnp.where(row % capacity == lane, by_slot, 0.0), axis=1, keepdims=True)
    gates = gates_ref[...].astype(f32)
    sums = jnp.concatenate(
        [
            jnp.sum(pick_first * gate, axis=0, keepdims=True),
            jnp.sum(pick_second * gate, axis=0, keepdims=True),
        ],
        axis=0,
    )
    dgate_ref[...] = (sums / gates).astype(bf16)


def finish_body(total_ref, gi_ref, go_ref):
    total = total_ref[...].astype(f32)
    gi_ref[...] = total[:LANES].T
    go_ref[...] = total[LANES:].T


def shards(tokens, out_grad, gates, expert_ids, w_in, w_out):
    tok_rows, width = tokens.shape
    experts = lax.axis_size("expert")
    replicas = lax.axis_size("dp")
    capacity = 3 * tok_rows // experts
    slots = experts * capacity
    tiles = width // LANES
    shard = w_in.shape[2]
    same_core = [[i for i in range(replicas) if i % 2 == c] for c in range(2)]
    swap = [(i, i ^ 1) for i in range(replicas)]
    sds = jax.ShapeDtypeStruct

    def send(value, perm):
        return lax.ppermute(value, "dp", perm)

    wi = w_in.reshape(width, shard)
    wo = w_out.reshape(width, shard)
    ids = expert_ids.T
    gates_row = gates.T

    weights = lax.all_gather(
        jnp.concatenate([wi, wo], axis=0), "dp", axis=0, tiled=False, axis_index_groups=same_core
    )

    payload = call(
        lambda *refs: dispatch_body(experts, capacity, *refs),
        sds((slots * 2 * tiles, LANES), bf16),
        "dispatch",
        [pltpu.VMEM((slots * 2 * tiles, LANES), f32)],
    )(ids, gates_row, tokens, out_grad)
    mine = lax.all_to_all(
        payload.reshape(experts, capacity * 2 * tiles, LANES),
        "expert", split_axis=0, concat_axis=0, tiled=True,
    ).reshape(slots * 2 * tiles, LANES)
    other = send(mine, swap)
    rows = sds((2 * slots, width), bf16)
    x, dy = call(
        unpack_body, (rows, rows), "unpack", [pltpu.VMEM((slots * 2 * tiles, LANES), f32)]
    )(mine, other)
    x, dy, weights = lax.optimization_barrier((x, dy, weights))
    blocks = replicas // 2
    d_pre, gate, grads = call(
        units_body,
        (
            sds((2 * slots, blocks * shard), bf16),
            sds((2 * slots, LANES), f32),
            sds((blocks, 2 * shard, width), bf16),
        ),
        "units",
    )(x, dy, weights)
    total = lax.psum_scatter(
        grads, "dp", scatter_dimension=0, tiled=False, axis_index_groups=same_core
    )
    keep, keep_gate, give = call(
        dx_body,
        (sds((slots, width), f32), sds((slots, LANES), f32), sds((slots, width + LANES), bf16)),
        "input_gradient",
    )(d_pre, weights, gate)
    took = send(give, swap)
    back = call(
        lambda *refs: pack_body(experts, capacity, *refs),
        sds((experts * (capacity + 1) * tiles, LANES), bf16),
        "pack",
        [
            pltpu.VMEM((tiles, slots, LANES), f32),
            pltpu.VMEM((experts * (capacity + 1) * tiles, LANES), f32),
        ],
    )(keep, keep_gate, took)
    back = lax.all_to_all(
        back.reshape(experts, (capacity + 1) * tiles, LANES),
        "expert", split_axis=0, concat_axis=0, tiled=True,
    ).reshape(experts * (capacity + 1) * tiles, LANES)
    d_tokens, gate_grad = call(
        lambda *refs: combine_body(experts, capacity, *refs),
        (sds((tok_rows, width), bf16), sds((2, tok_rows), bf16)),
        "combine",
        [
            pltpu.VMEM((experts * (capacity + 1) * tiles, LANES), f32),
            pltpu.VMEM((tiles, slots, LANES), f32),
        ],
    )(ids, gates_row, back)
    d_tokens, gate_grad, total = lax.optimization_barrier((d_tokens, gate_grad, total))
    own = sds((width, shard), f32)
    grad_in, grad_out = call(finish_body, (own, own), "finish")(total)
    return d_tokens, gate_grad.T, grad_in[None], grad_out[None]


def solution(mesh):
    by_token = P(("dp", "expert"), None)
    by_expert = P("expert", None, "dp")
    return jax.shard_map(
        shards,
        mesh=mesh,
        in_specs=(by_token, by_token, by_token, by_token, by_expert, by_expert),
        out_specs=(by_token, by_token, by_expert, by_expert),
        check_vma=False,
    )
```

```python
import jax
import jax.numpy as jnp
from jax import lax
from jax.experimental import pallas as pl
from jax.experimental.pallas import tpu as pltpu
from jax.sharding import PartitionSpec as P

gelu_scale = 0.7978845608028654
cubic_coef = 0.044715
bf16 = jnp.bfloat16
f32 = jnp.float32
LANES = 128
VMEM_BYTES = 56 << 20


def call(body, out_shape, name, scratch=(), scalars=0, arrays=0):
    specs = {}
    if scalars:
        specs["in_specs"] = [pl.BlockSpec(memory_space=pltpu.SMEM)] * scalars + [
            pl.BlockSpec(memory_space=pltpu.VMEM)
        ] * arrays
    return pl.pallas_call(
        body,
        out_shape=out_shape,
        **specs,
        scratch_shapes=scratch,
        name=name,
        compiler_params=pltpu.CompilerParams(vmem_limit_bytes=VMEM_BYTES),
    )


def slot_targets(ids_ref, plane, experts, capacity):
    tokens = ids_ref.shape[1]

    def near_order(expert):
        up = (((expert >> 2) & 3) - plane) & 3
        return up * 16 + (expert >> 4) * 4 + (expert & 3)

    first = near_order(ids_ref[0:1, :])
    second = near_order(ids_ref[1:2, :])
    expert = lax.broadcasted_iota(jnp.int32, (experts, tokens), 0)
    is_first = (expert == first).astype(f32)
    is_second = (expert == second).astype(f32)
    before = (
        lax.broadcasted_iota(jnp.int32, (tokens, tokens), 0)
        < lax.broadcasted_iota(jnp.int32, (tokens, tokens), 1)
    ).astype(f32)
    earlier = jnp.dot(
        (is_first + is_second).astype(bf16), before.astype(bf16), preferred_element_type=f32
    )
    slot_first = jnp.sum(earlier * is_first, axis=0, keepdims=True).astype(jnp.int32)
    slot_second = jnp.sum(earlier * is_second, axis=0, keepdims=True).astype(jnp.int32)
    return first * capacity + slot_first, second * capacity + slot_second


def one_hots(ids_ref, plane, experts, capacity):
    tokens = ids_ref.shape[1]
    first, second = slot_targets(ids_ref, plane, experts, capacity)
    slot = lax.broadcasted_iota(jnp.int32, (experts * capacity, tokens), 0)
    return (slot == first).astype(f32), (slot == second).astype(f32)


def dispatch_body(experts, capacity, plane_ref, ids_ref, gates_ref, x_ref, dy_ref, *refs):
    out_refs, wide_ref = refs[:-1], refs[-1]
    width = x_ref.shape[1] // LANES
    slots = experts * capacity
    pick_first, pick_second = one_hots(ids_ref, plane_ref[0], experts, capacity)
    gates = gates_ref[...].astype(f32)
    pick = (pick_first + pick_second).astype(bf16)
    gated = (pick_first * gates[0:1, :] + pick_second * gates[1:2, :]).astype(bf16)
    rows_x = jnp.dot(pick, x_ref[...], preferred_element_type=f32)
    rows_dy = jnp.dot(gated, dy_ref[...], preferred_element_type=f32)
    for j in range(width):
        cols = slice(j * LANES, (j + 1) * LANES)
        wide_ref[pl.ds(j, slots, stride=2 * width), :] = rows_x[:, cols]
        wide_ref[pl.ds(width + j, slots, stride=2 * width), :] = rows_dy[:, cols]
    part = slots * 2 * width // len(out_refs)
    for i, out_ref in enumerate(out_refs):
        out_ref[...] = wide_ref[i * part : (i + 1) * part].astype(bf16)


def gelu_parts(pre):
    inner = jnp.tanh(gelu_scale * (pre + cubic_coef * pre * pre * pre))
    value = 0.5 * pre * (1.0 + inner)
    slope = 0.5 * (1.0 + inner) + 0.5 * pre * (1.0 - inner * inner) * gelu_scale * (
        1.0 + 3.0 * cubic_coef * pre * pre
    )
    return value, slope


def unpack(got_ref, x_ref, dy_ref, wide_ref):
    slots = x_ref.shape[0]
    width = x_ref.shape[1] // LANES
    wide_ref[...] = got_ref[...].astype(f32)
    for j in range(width):
        cols = slice(j * LANES, (j + 1) * LANES)
        x_ref[:, cols] = wide_ref[pl.ds(j, slots, stride=2 * width), :].astype(bf16)
        dy_ref[:, cols] = wide_ref[pl.ds(width + j, slots, stride=2 * width), :].astype(bf16)


def project(x, dy, w_ref, dpre_ref, act_ref, gate_ref):
    width = x.shape[1]
    gates = []
    for pair in range(0, w_ref.shape[0], 2):
        cols = slice(pair * LANES, (pair + 2) * LANES)
        w_first = jnp.concatenate([w_ref[pair, :width], w_ref[pair + 1, :width]], axis=1)
        w_second = jnp.concatenate([w_ref[pair, width:], w_ref[pair + 1, width:]], axis=1)
        pre = jnp.dot(x, w_first, preferred_element_type=f32)
        dy_proj = jnp.dot(dy, w_second, preferred_element_type=f32)
        value, slope = gelu_parts(pre)
        activated = value.astype(bf16)
        gate = activated.astype(f32) * dy_proj
        gates += [gate[:, :LANES], gate[:, LANES:]]
        dpre_ref[:, cols] = (dy_proj * slope).astype(bf16)
        act_ref[:, cols] = activated
    gate_ref[...] = sum(gates[1:], gates[0])


def mine_body(x_ref, dy_ref, w_ref, dpre_ref, act_ref, gate_ref):
    project(x_ref[...], dy_ref[...], w_ref, dpre_ref, act_ref, gate_ref)


def other_body(
    got_ref, x_ref, dy_ref, dpre_in_ref, act_in_ref, w_ref,
    dpre_ref, gate_ref, grad_ref, wide_ref, xo_ref, dyo_ref, act_ref,
):
    unpack(got_ref, xo_ref, dyo_ref, wide_ref)
    project(xo_ref[...], dyo_ref[...], w_ref, dpre_ref, act_ref, gate_ref)
    for row, sides in (
        (0, ((dpre_in_ref, x_ref), (dpre_ref, xo_ref))),
        (LANES, ((act_in_ref, dy_ref), (act_ref, dyo_ref))),
    ):
        for pair in range(0, w_ref.shape[0], 2):
            cols = slice(pair * LANES, (pair + 2) * LANES)
            grad = sum(
                lax.dot_general(
                    left[:, cols], right[...], (((0,), (0,)), ((), ())), preferred_element_type=f32
                )
                for left, right in sides
            ).astype(bf16)
            grad_ref[pair, row : row + LANES] = grad[:LANES]
            grad_ref[pair + 1, row : row + LANES] = grad[LANES:]


def dx_body(dpre_m, dpre_o, w_ref, gate_m, gate_o, keep_ref, keep_gate_ref, give_ref):
    slots = keep_ref.shape[0]
    width = keep_ref.shape[1]
    weights = jnp.concatenate([w_ref[i, :width] for i in range(w_ref.shape[0])], axis=1)
    dims = (((1,), (1,)), ((), ()))
    give = lax.dot_general(dpre_o[...], weights, dims, preferred_element_type=f32)
    give_ref[:, :width] = give.astype(bf16)
    keep_ref[...] = lax.dot_general(dpre_m[...], weights, dims, preferred_element_type=f32)
    gate = jnp.sum(gate_m[...], axis=1, keepdims=True)
    keep_gate_ref[...] = jnp.broadcast_to(gate, keep_gate_ref.shape)
    gate = jnp.sum(gate_o[...], axis=1, keepdims=True)
    coarse = gate.astype(bf16).astype(f32)
    fine = (gate - coarse).astype(bf16).astype(f32)
    lane = lax.broadcasted_iota(jnp.int32, (slots, LANES), 1)
    give_ref[:, width:] = jnp.where(
        lane == 0, coarse, jnp.where(lane == 1, fine, 0.0)
    ).astype(bf16)


def pack_body(experts, capacity, keep_ref, keep_gate_ref, took_ref, out_ref, rows_ref, wide_ref):
    slots = keep_ref.shape[0]
    width = keep_ref.shape[1]
    tiles = width // LANES
    step = (capacity + 1) * tiles
    for j in range(tiles):
        cols = slice(j * LANES, (j + 1) * LANES)
        total = keep_ref[:, cols] + took_ref[:, cols].astype(f32)
        rows_ref[j] = total.astype(bf16).astype(f32)
    gate = keep_gate_ref[:, 0:1] + jnp.sum(took_ref[:, width:].astype(f32), axis=1, keepdims=True)
    row = lax.broadcasted_iota(jnp.int32, (slots, LANES), 0)
    lane = lax.broadcasted_iota(jnp.int32, (slots, LANES), 1)
    spread = jnp.where(row % capacity == lane, gate, 0.0).astype(bf16)
    expert = lax.broadcasted_iota(jnp.int32, (experts, slots), 0)
    slot = lax.broadcasted_iota(jnp.int32, (experts, slots), 1)
    owner = (slot // capacity == expert).astype(f32).astype(bf16)
    table = jnp.dot(owner, spread, preferred_element_type=f32)
    for c in range(capacity):
        for j in range(tiles):
            wide_ref[pl.ds(c * tiles + j, experts, stride=step), :] = rows_ref[
                j, pl.ds(c, experts, stride=capacity), :
            ]
    for j in range(tiles):
        wide_ref[pl.ds(capacity * tiles + j, experts, stride=step), :] = (
            table if j == 0 else jnp.zeros_like(table)
        )
    out_ref[...] = wide_ref[...].astype(bf16)


def combine_body(
    experts, capacity, plane_ref, ids_ref, gates_ref, b0, b1, b2, b3,
    dtok_ref, dgate_ref, wide_ref, rows_ref,
):
    slots = experts * capacity
    tiles = dtok_ref.shape[1] // LANES
    step = (capacity + 1) * tiles
    for i, ref in enumerate((b0, b1, b2, b3)):
        part = ref.shape[0]
        wide_ref[i * part : (i + 1) * part] = ref[...].astype(f32)
    for c in range(capacity):
        for j in range(tiles):
            rows_ref[j, pl.ds(c, experts, stride=capacity), :] = wide_ref[
                pl.ds(c * tiles + j, experts, stride=step), :
            ]
    table = wide_ref[pl.ds(capacity * tiles, experts, stride=step), :].astype(bf16)
    pick_first, pick_second = one_hots(ids_ref, plane_ref[0], experts, capacity)
    pick = (pick_first + pick_second).astype(bf16)
    for j in range(tiles):
        dtok_ref[:, j * LANES : (j + 1) * LANES] = lax.dot_general(
            pick, rows_ref[j].astype(bf16), (((0,), (0,)), ((), ())), preferred_element_type=f32
        ).astype(bf16)
    expert = lax.broadcasted_iota(jnp.int32, (slots, experts), 1)
    slot = lax.broadcasted_iota(jnp.int32, (slots, experts), 0)
    owner = (slot // capacity == expert).astype(f32).astype(bf16)
    by_slot = jnp.dot(owner, table, preferred_element_type=f32)
    row = lax.broadcasted_iota(jnp.int32, (slots, LANES), 0)
    lane = lax.broadcasted_iota(jnp.int32, (slots, LANES), 1)
    gate = jnp.sum(jnp.where(row % capacity == lane, by_slot, 0.0), axis=1, keepdims=True)
    gates = gates_ref[...].astype(f32)
    sums = jnp.concatenate(
        [
            jnp.sum(pick_first * gate, axis=0, keepdims=True),
            jnp.sum(pick_second * gate, axis=0, keepdims=True),
        ],
        axis=0,
    )
    dgate_ref[...] = (sums / gates).astype(bf16)


def finish_body(total_ref, gi_ref, go_ref):
    total = total_ref[...].astype(f32)
    gi_ref[...] = total[:LANES].T
    go_ref[...] = total[LANES:].T


def shards(tokens, out_grad, gates, expert_ids, w_in, w_out):
    tok_rows, width = tokens.shape
    experts = lax.axis_size("expert")
    replicas = lax.axis_size("dp")
    capacity = 3 * tok_rows // experts
    slots = experts * capacity
    tiles = width // LANES
    shard = w_in.shape[2]
    same_core = [[i for i in range(replicas) if i % 2 == c] for c in range(2)]
    swap = [(i, i ^ 1) for i in range(replicas)]
    sds = jax.ShapeDtypeStruct

    plane = ((lax.axis_index("expert") >> 2) & 3).astype(jnp.int32).reshape(1)
    in_plane = [[x * 16 + zl * 4 + y for x in range(4) for y in range(4)] for zl in range(4)]

    def device(z, core, x, y):
        return ((z >> 2) * 2 + core) * experts + x * 16 + (z & 3) * 4 + y

    def along_z(hops):
        length = 2 * replicas
        return [
            (device(z, c, x, y), device((z + hops(z)) % length, c, x, y))
            for z in range(length) for c in range(2) for x in range(4) for y in range(4)
        ]

    out_perms = [along_z(lambda z: 1), along_z(lambda z: -2 if z % 2 else 2), along_z(lambda z: -1)]
    home_perms = [[(b, a) for a, b in perm] for perm in out_perms]

    def move(values, perms):
        return values[:1] + [
            lax.ppermute(v, ("dp", "expert"), perm) for v, perm in zip(values[1:], perms)
        ]

    def send(value, perm):
        return lax.ppermute(value, "dp", perm)

    wi = w_in.reshape(width, shard)
    wo = w_out.reshape(width, shard)
    ids = expert_ids.T
    gates_row = gates.T

    weights = lax.all_gather(
        jnp.concatenate([wi, wo], axis=0), "dp", axis=0, tiled=False, axis_index_groups=same_core
    )

    chunk = capacity * 2 * tiles
    quarter = sds((slots * 2 * tiles // 4, LANES), bf16)
    payload = call(
        lambda *refs: dispatch_body(experts, capacity, *refs),
        (quarter,) * 4,
        "dispatch",
        [pltpu.VMEM((slots * 2 * tiles, LANES), f32)],
        1,
        4,
    )(plane, ids, gates_row, tokens, out_grad)
    payload = move(list(payload), out_perms)
    mine = lax.all_to_all(
        jnp.concatenate([v.reshape(experts // 4, chunk, LANES) for v in payload], axis=1),
        "expert", split_axis=0, concat_axis=0, tiled=True, axis_index_groups=in_plane,
    ).reshape(slots * 2 * tiles, LANES)
    rows = sds((slots, width), bf16)
    wide = pltpu.VMEM((slots * 2 * tiles, LANES), f32)
    x, dy = call(unpack, (rows, rows), "unpack", [wide])(mine)
    mine, x, dy, weights = lax.optimization_barrier((mine, x, dy, weights))
    other = send(mine, swap)
    blocks = replicas // 2
    hidden = sds((slots, blocks * shard), bf16)
    gate_shape = sds((slots, LANES), f32)
    dpre_mine, act_mine, gate_mine = call(mine_body, (hidden, hidden, gate_shape), "mine")(
        x, dy, weights
    )
    dpre_other, gate_other, grads = call(
        other_body,
        (hidden, gate_shape, sds((blocks, 2 * shard, width), bf16)),
        "other",
        [
            wide,
            pltpu.VMEM((slots, width), bf16),
            pltpu.VMEM((slots, width), bf16),
            pltpu.VMEM((slots, blocks * shard), bf16),
        ],
    )(other, x, dy, dpre_mine, act_mine, weights)
    total = lax.psum_scatter(
        grads, "dp", scatter_dimension=0, tiled=False, axis_index_groups=same_core
    )
    keep, keep_gate, give = call(
        dx_body,
        (sds((slots, width), f32), sds((slots, LANES), f32), sds((slots, width + LANES), bf16)),
        "input_gradient",
    )(dpre_mine, dpre_other, weights, gate_mine, gate_other)
    took = send(give, swap)
    back = call(
        lambda *refs: pack_body(experts, capacity, *refs),
        sds((experts * (capacity + 1) * tiles, LANES), bf16),
        "pack",
        [
            pltpu.VMEM((tiles, slots, LANES), f32),
            pltpu.VMEM((experts * (capacity + 1) * tiles, LANES), f32),
        ],
    )(keep, keep_gate, took)
    chunk = (capacity + 1) * tiles
    back = lax.all_to_all(
        back.reshape(experts // 4, 4 * chunk, LANES),
        "expert", split_axis=0, concat_axis=0, tiled=True, axis_index_groups=in_plane,
    )
    back = move(
        [
            back[:, i * chunk : (i + 1) * chunk].reshape(experts // 4 * chunk, LANES)
            for i in range(4)
        ],
        home_perms,
    )
    d_tokens, gate_grad = call(
        lambda *refs: combine_body(experts, capacity, *refs),
        (sds((tok_rows, width), bf16), sds((2, tok_rows), bf16)),
        "combine",
        [
            pltpu.VMEM((experts * (capacity + 1) * tiles, LANES), f32),
            pltpu.VMEM((tiles, slots, LANES), f32),
        ],
        1,
        6,
    )(plane, ids, gates_row, *back)
    d_tokens, gate_grad, total = lax.optimization_barrier((d_tokens, gate_grad, total))
    own = sds((width, shard), f32)
    grad_in, grad_out = call(finish_body, (own, own), "finish")(total)
    return d_tokens, gate_grad.T, grad_in[None], grad_out[None]


def solution(mesh):
    by_token = P(("dp", "expert"), None)
    by_expert = P("expert", None, "dp")
    return jax.shard_map(
        shards,
        mesh=mesh,
        in_specs=(by_token, by_token, by_token, by_token, by_expert, by_expert),
        out_specs=(by_token, by_token, by_expert, by_expert),
        check_vma=False,
    )
```

```python
import jax
import jax.numpy as jnp
from jax import lax
from jax.experimental import pallas as pl
from jax.experimental.pallas import tpu as pltpu
from jax.sharding import PartitionSpec as P

gelu_scale = 0.7978845608028654
cubic_coef = 0.044715
bf16 = jnp.bfloat16
f32 = jnp.float32
LANES = 128
VMEM_BYTES = 56 << 20


def call(body, out_shape, name, scratch=(), scalars=0, arrays=0):
    specs = {}
    if scalars:
        specs["in_specs"] = [pl.BlockSpec(memory_space=pltpu.SMEM)] * scalars + [
            pl.BlockSpec(memory_space=pltpu.VMEM)
        ] * arrays
    return pl.pallas_call(
        body,
        out_shape=out_shape,
        **specs,
        scratch_shapes=scratch,
        name=name,
        compiler_params=pltpu.CompilerParams(vmem_limit_bytes=VMEM_BYTES),
    )


def slot_targets(ids_ref, plane, experts, capacity, planes_first):
    tokens = ids_ref.shape[1]

    def near_order(expert):
        up = (((expert >> 2) & 3) - plane) & 3
        place = (expert >> 4) * 4 + (expert & 3)
        return up * 16 + place if planes_first else place * 4 + up

    first = near_order(ids_ref[0:1, :])
    second = near_order(ids_ref[1:2, :])
    expert = lax.broadcasted_iota(jnp.int32, (experts, tokens), 0)
    is_first = (expert == first).astype(f32)
    is_second = (expert == second).astype(f32)
    before = (
        lax.broadcasted_iota(jnp.int32, (tokens, tokens), 0)
        < lax.broadcasted_iota(jnp.int32, (tokens, tokens), 1)
    ).astype(f32)
    earlier = jnp.dot(
        (is_first + is_second).astype(bf16), before.astype(bf16), preferred_element_type=f32
    )
    slot_first = jnp.sum(earlier * is_first, axis=0, keepdims=True).astype(jnp.int32)
    slot_second = jnp.sum(earlier * is_second, axis=0, keepdims=True).astype(jnp.int32)
    return first * capacity + slot_first, second * capacity + slot_second


def one_hots(ids_ref, plane, experts, capacity, planes_first):
    tokens = ids_ref.shape[1]
    first, second = slot_targets(ids_ref, plane, experts, capacity, planes_first)
    slot = lax.broadcasted_iota(jnp.int32, (experts * capacity, tokens), 0)
    return (slot == first).astype(f32), (slot == second).astype(f32)


def dispatch_body(experts, capacity, plane_ref, ids_ref, gates_ref, x_ref, dy_ref, out_ref, wide_ref):
    width = x_ref.shape[1] // LANES
    slots = experts * capacity
    pick_first, pick_second = one_hots(ids_ref, plane_ref[0], experts, capacity, False)
    gates = gates_ref[...].astype(f32)
    pick = (pick_first + pick_second).astype(bf16)
    gated = (pick_first * gates[0:1, :] + pick_second * gates[1:2, :]).astype(bf16)
    rows_x = jnp.dot(pick, x_ref[...], preferred_element_type=f32)
    rows_dy = jnp.dot(gated, dy_ref[...], preferred_element_type=f32)
    for j in range(width):
        cols = slice(j * LANES, (j + 1) * LANES)
        wide_ref[pl.ds(j, slots, stride=2 * width), :] = rows_x[:, cols]
        wide_ref[pl.ds(width + j, slots, stride=2 * width), :] = rows_dy[:, cols]
    out_ref[...] = wide_ref[...].astype(bf16)


def gelu_parts(pre):
    inner = jnp.tanh(gelu_scale * (pre + cubic_coef * pre * pre * pre))
    value = 0.5 * pre * (1.0 + inner)
    slope = 0.5 * (1.0 + inner) + 0.5 * pre * (1.0 - inner * inner) * gelu_scale * (
        1.0 + 3.0 * cubic_coef * pre * pre
    )
    return value, slope


def unpack_body(r0, r1, r2, r3, rows_ref, wide_ref):
    slots, width = rows_ref.shape
    tiles = width // LANES
    for i, ref in enumerate((r0, r1, r2, r3)):
        part = ref.shape[0]
        wide_ref[i * part : (i + 1) * part] = ref[...].astype(f32)
    for j in range(tiles):
        rows_ref[:, j * LANES : (j + 1) * LANES] = wide_ref[
            pl.ds(j, slots, stride=tiles), :
        ].astype(bf16)


def project(rows_ref, w_ref, dpre_ref, act_ref, gate_ref):
    width = rows_ref.shape[1] // 2
    x = rows_ref[:, :width]
    dy = rows_ref[:, width:]
    gates = []
    for pair in range(0, w_ref.shape[0], 2):
        cols = slice(pair * LANES, (pair + 2) * LANES)
        w_first = jnp.concatenate([w_ref[pair, :width], w_ref[pair + 1, :width]], axis=1)
        w_second = jnp.concatenate([w_ref[pair, width:], w_ref[pair + 1, width:]], axis=1)
        pre = jnp.dot(x, w_first, preferred_element_type=f32)
        dy_proj = jnp.dot(dy, w_second, preferred_element_type=f32)
        value, slope = gelu_parts(pre)
        activated = value.astype(bf16)
        gate = activated.astype(f32) * dy_proj
        gates += [gate[:, :LANES], gate[:, LANES:]]
        dpre_ref[:, cols] = (dy_proj * slope).astype(bf16)
        act_ref[:, cols] = activated
    gate_ref[...] = sum(gates[1:], gates[0])


def other_body(
    mine_ref, other_ref, dpre_in_ref, act_in_ref, w_ref, dpre_ref, gate_ref, grad_ref, act_ref
):
    width = mine_ref.shape[1] // 2
    project(other_ref, w_ref, dpre_ref, act_ref, gate_ref)
    for row, sides in (
        (0, ((dpre_in_ref, mine_ref), (dpre_ref, other_ref))),
        (LANES, ((act_in_ref, mine_ref), (act_ref, other_ref))),
    ):
        for pair in range(0, w_ref.shape[0], 2):
            cols = slice(pair * LANES, (pair + 2) * LANES)
            grad = sum(
                lax.dot_general(
                    left[:, cols],
                    right[:, width:] if row else right[:, :width],
                    (((0,), (0,)), ((), ())),
                    preferred_element_type=f32,
                )
                for left, right in sides
            ).astype(bf16)
            grad_ref[pair, row : row + LANES] = grad[:LANES]
            grad_ref[pair + 1, row : row + LANES] = grad[LANES:]


def dx_body(dpre_m, dpre_o, w_ref, gate_m, gate_o, keep_ref, keep_gate_ref, give_ref):
    slots = keep_ref.shape[0]
    width = keep_ref.shape[1]
    weights = jnp.concatenate([w_ref[i, :width] for i in range(w_ref.shape[0])], axis=1)
    dims = (((1,), (1,)), ((), ()))
    give = lax.dot_general(dpre_o[...], weights, dims, preferred_element_type=f32)
    give_ref[:, :width] = give.astype(bf16)
    keep_ref[...] = lax.dot_general(dpre_m[...], weights, dims, preferred_element_type=f32)
    gate = jnp.sum(gate_m[...], axis=1, keepdims=True)
    keep_gate_ref[...] = jnp.broadcast_to(gate, keep_gate_ref.shape)
    gate = jnp.sum(gate_o[...], axis=1, keepdims=True)
    coarse = gate.astype(bf16).astype(f32)
    fine = (gate - coarse).astype(bf16).astype(f32)
    lane = lax.broadcasted_iota(jnp.int32, (slots, LANES), 1)
    give_ref[:, width:] = jnp.where(
        lane == 0, coarse, jnp.where(lane == 1, fine, 0.0)
    ).astype(bf16)


def pack_body(experts, capacity, keep_ref, keep_gate_ref, took_ref, out_ref, rows_ref, wide_ref):
    slots = keep_ref.shape[0]
    width = keep_ref.shape[1]
    tiles = width // LANES
    step = (capacity + 1) * tiles
    for j in range(tiles):
        cols = slice(j * LANES, (j + 1) * LANES)
        total = keep_ref[:, cols] + took_ref[:, cols].astype(f32)
        rows_ref[j] = total.astype(bf16).astype(f32)
    gate = keep_gate_ref[:, 0:1] + jnp.sum(took_ref[:, width:].astype(f32), axis=1, keepdims=True)
    row = lax.broadcasted_iota(jnp.int32, (slots, LANES), 0)
    lane = lax.broadcasted_iota(jnp.int32, (slots, LANES), 1)
    spread = jnp.where(row % capacity == lane, gate, 0.0).astype(bf16)
    expert = lax.broadcasted_iota(jnp.int32, (experts, slots), 0)
    slot = lax.broadcasted_iota(jnp.int32, (experts, slots), 1)
    owner = (slot // capacity == expert).astype(f32).astype(bf16)
    table = jnp.dot(owner, spread, preferred_element_type=f32)
    for c in range(capacity):
        for j in range(tiles):
            wide_ref[pl.ds(c * tiles + j, experts, stride=step), :] = rows_ref[
                j, pl.ds(c, experts, stride=capacity), :
            ]
    for j in range(tiles):
        wide_ref[pl.ds(capacity * tiles + j, experts, stride=step), :] = (
            table if j == 0 else jnp.zeros_like(table)
        )
    places = out_ref.shape[0]
    planes = experts // places
    for i in range(planes):
        part = wide_ref[i * places * step : (i + 1) * places * step]
        out_ref[:, i * step : (i + 1) * step] = part.reshape(places, step, LANES).astype(bf16)


def combine_body(
    experts, capacity, plane_ref, ids_ref, gates_ref, b0, b1, b2, b3,
    dtok_ref, dgate_ref, wide_ref, rows_ref,
):
    slots = experts * capacity
    tiles = dtok_ref.shape[1] // LANES
    step = (capacity + 1) * tiles
    for i, ref in enumerate((b0, b1, b2, b3)):
        part = ref.shape[0]
        wide_ref[i * part : (i + 1) * part] = ref[...].astype(f32)
    for c in range(capacity):
        for j in range(tiles):
            rows_ref[j, pl.ds(c, experts, stride=capacity), :] = wide_ref[
                pl.ds(c * tiles + j, experts, stride=step), :
            ]
    table = wide_ref[pl.ds(capacity * tiles, experts, stride=step), :].astype(bf16)
    pick_first, pick_second = one_hots(ids_ref, plane_ref[0], experts, capacity, True)
    pick = (pick_first + pick_second).astype(bf16)
    for j in range(tiles):
        dtok_ref[:, j * LANES : (j + 1) * LANES] = lax.dot_general(
            pick, rows_ref[j].astype(bf16), (((0,), (0,)), ((), ())), preferred_element_type=f32
        ).astype(bf16)
    expert = lax.broadcasted_iota(jnp.int32, (slots, experts), 1)
    slot = lax.broadcasted_iota(jnp.int32, (slots, experts), 0)
    owner = (slot // capacity == expert).astype(f32).astype(bf16)
    by_slot = jnp.dot(owner, table, preferred_element_type=f32)
    row = lax.broadcasted_iota(jnp.int32, (slots, LANES), 0)
    lane = lax.broadcasted_iota(jnp.int32, (slots, LANES), 1)
    gate = jnp.sum(jnp.where(row % capacity == lane, by_slot, 0.0), axis=1, keepdims=True)
    gates = gates_ref[...].astype(f32)
    sums = jnp.concatenate(
        [
            jnp.sum(pick_first * gate, axis=0, keepdims=True),
            jnp.sum(pick_second * gate, axis=0, keepdims=True),
        ],
        axis=0,
    )
    dgate_ref[...] = (sums / gates).astype(bf16)


def finish_body(total_ref, gi_ref, go_ref):
    total = total_ref[...].astype(f32)
    gi_ref[...] = total[:LANES].T
    go_ref[...] = total[LANES:].T


def shards(tokens, out_grad, gates, expert_ids, w_in, w_out):
    tok_rows, width = tokens.shape
    experts = lax.axis_size("expert")
    replicas = lax.axis_size("dp")
    capacity = 3 * tok_rows // experts
    slots = experts * capacity
    tiles = width // LANES
    shard = w_in.shape[2]
    same_core = [[i for i in range(replicas) if i % 2 == c] for c in range(2)]
    swap = [(i, i ^ 1) for i in range(replicas)]
    sds = jax.ShapeDtypeStruct

    plane = ((lax.axis_index("expert") >> 2) & 3).astype(jnp.int32).reshape(1)
    in_plane = [[x * 16 + zl * 4 + y for x in range(4) for y in range(4)] for zl in range(4)]

    def device(z, core, x, y):
        return ((z >> 2) * 2 + core) * experts + x * 16 + (z & 3) * 4 + y

    def along_z(hops):
        length = 2 * replicas
        return [
            (device(z, c, x, y), device((z + hops(z)) % length, c, x, y))
            for z in range(length) for c in range(2) for x in range(4) for y in range(4)
        ]

    out_perms = [along_z(lambda z: 1), along_z(lambda z: -2 if z % 2 else 2), along_z(lambda z: -1)]
    home_perms = [[(b, a) for a, b in perm] for perm in out_perms]

    def move(values, perms):
        return values[:1] + [
            lax.ppermute(v, ("dp", "expert"), perm) for v, perm in zip(values[1:], perms)
        ]

    def by_plane(array, rows):
        return [
            array[:, i * rows : (i + 1) * rows].reshape(experts // 4 * rows, LANES)
            for i in range(4)
        ]

    def send(value, perm):
        return lax.ppermute(value, "dp", perm)

    wi = w_in.reshape(width, shard)
    wo = w_out.reshape(width, shard)
    ids = expert_ids.T
    gates_row = gates.T

    weights = lax.all_gather(
        jnp.concatenate([wi, wo], axis=0), "dp", axis=0, tiled=False, axis_index_groups=same_core
    )

    chunk = capacity * 2 * tiles
    wide = pltpu.VMEM((slots * 2 * tiles, LANES), f32)
    payload = call(
        lambda *refs: dispatch_body(experts, capacity, *refs),
        sds((slots * 2 * tiles, LANES), bf16),
        "dispatch",
        [wide],
        1,
        4,
    )(plane, ids, gates_row, tokens, out_grad)
    got = lax.all_to_all(
        payload.reshape(experts // 4, 4 * chunk, LANES),
        "expert", split_axis=0, concat_axis=0, tiled=True, axis_index_groups=in_plane,
    )
    got = move(by_plane(got, chunk), out_perms)
    mine = call(unpack_body, sds((slots, 2 * width), bf16), "unpack", [wide])(*got)
    mine, weights = lax.optimization_barrier((mine, weights))
    other = send(mine, swap)
    blocks = replicas // 2
    hidden = sds((slots, blocks * shard), bf16)
    gate_shape = sds((slots, LANES), f32)
    dpre_mine, act_mine, gate_mine = call(project, (hidden, hidden, gate_shape), "mine")(
        mine, weights
    )
    dpre_other, gate_other, grads = call(
        other_body,
        (hidden, gate_shape, sds((blocks, 2 * shard, width), bf16)),
        "other",
        [pltpu.VMEM((slots, blocks * shard), bf16)],
    )(mine, other, dpre_mine, act_mine, weights)
    total = lax.psum_scatter(
        grads, "dp", scatter_dimension=0, tiled=False, axis_index_groups=same_core
    )
    keep, keep_gate, give = call(
        dx_body,
        (sds((slots, width), f32), sds((slots, LANES), f32), sds((slots, width + LANES), bf16)),
        "input_gradient",
    )(dpre_mine, dpre_other, weights, gate_mine, gate_other)
    took = send(give, swap)
    back = call(
        lambda *refs: pack_body(experts, capacity, *refs),
        sds((experts // 4, 4 * (capacity + 1) * tiles, LANES), bf16),
        "pack",
        [
            pltpu.VMEM((tiles, slots, LANES), f32),
            pltpu.VMEM((experts * (capacity + 1) * tiles, LANES), f32),
        ],
    )(keep, keep_gate, took)
    chunk = (capacity + 1) * tiles
    back = lax.all_to_all(
        back,
        "expert", split_axis=0, concat_axis=0, tiled=True, axis_index_groups=in_plane,
    )
    back = move(by_plane(back, chunk), home_perms)
    d_tokens, gate_grad = call(
        lambda *refs: combine_body(experts, capacity, *refs),
        (sds((tok_rows, width), bf16), sds((2, tok_rows), bf16)),
        "combine",
        [
            pltpu.VMEM((experts * (capacity + 1) * tiles, LANES), f32),
            pltpu.VMEM((tiles, slots, LANES), f32),
        ],
        1,
        6,
    )(plane, ids, gates_row, *back)
    d_tokens, gate_grad, total = lax.optimization_barrier((d_tokens, gate_grad, total))
    own = sds((width, shard), f32)
    grad_in, grad_out = call(finish_body, (own, own), "finish")(total)
    return d_tokens, gate_grad.T, grad_in[None], grad_out[None]


def solution(mesh):
    by_token = P(("dp", "expert"), None)
    by_expert = P("expert", None, "dp")
    return jax.shard_map(
        shards,
        mesh=mesh,
        in_specs=(by_token, by_token, by_token, by_token, by_expert, by_expert),
        out_specs=(by_token, by_token, by_expert, by_expert),
        check_vma=False,
    )
```

```python
import jax
import jax.numpy as jnp
from jax import lax
from jax.experimental import pallas as pl
from jax.experimental.pallas import tpu as pltpu
from jax.sharding import PartitionSpec as P

gelu_scale = 0.7978845608028654
cubic_coef = 0.044715
bf16 = jnp.bfloat16
f32 = jnp.float32
LANES = 128
VMEM_BYTES = 56 << 20


def call(body, out_shape, name, scratch=(), scalars=0, arrays=0):
    specs = {}
    if scalars:
        specs["in_specs"] = [pl.BlockSpec(memory_space=pltpu.SMEM)] * scalars + [
            pl.BlockSpec(memory_space=pltpu.VMEM)
        ] * arrays
    return pl.pallas_call(
        body,
        out_shape=out_shape,
        **specs,
        scratch_shapes=scratch,
        name=name,
        compiler_params=pltpu.CompilerParams(vmem_limit_bytes=VMEM_BYTES),
    )


def slot_targets(ids_ref, plane, experts, capacity, planes_first):
    tokens = ids_ref.shape[1]

    def near_order(expert):
        up = (((expert >> 2) & 3) - plane) & 3
        place = (expert >> 4) * 4 + (expert & 3)
        return up * 16 + place if planes_first else place * 4 + up

    first = near_order(ids_ref[0:1, :])
    second = near_order(ids_ref[1:2, :])
    expert = lax.broadcasted_iota(jnp.int32, (experts, tokens), 0)
    is_first = (expert == first).astype(f32)
    is_second = (expert == second).astype(f32)
    before = (
        lax.broadcasted_iota(jnp.int32, (tokens, tokens), 0)
        < lax.broadcasted_iota(jnp.int32, (tokens, tokens), 1)
    ).astype(f32)
    earlier = jnp.dot(
        (is_first + is_second).astype(bf16), before.astype(bf16), preferred_element_type=f32
    )
    slot_first = jnp.sum(earlier * is_first, axis=0, keepdims=True).astype(jnp.int32)
    slot_second = jnp.sum(earlier * is_second, axis=0, keepdims=True).astype(jnp.int32)
    return first * capacity + slot_first, second * capacity + slot_second


def one_hots(ids_ref, plane, experts, capacity, planes_first):
    tokens = ids_ref.shape[1]
    first, second = slot_targets(ids_ref, plane, experts, capacity, planes_first)
    slot = lax.broadcasted_iota(jnp.int32, (experts * capacity, tokens), 0)
    return (slot == first).astype(f32), (slot == second).astype(f32)


def dispatch_body(experts, capacity, plane_ref, ids_ref, gates_ref, x_ref, dy_ref, out_ref, wide_ref):
    width = x_ref.shape[1] // LANES
    slots = experts * capacity
    pick_first, pick_second = one_hots(ids_ref, plane_ref[0], experts, capacity, False)
    gates = gates_ref[...].astype(f32)
    pick = (pick_first + pick_second).astype(bf16)
    gated = (pick_first * gates[0:1, :] + pick_second * gates[1:2, :]).astype(bf16)
    rows_x = jnp.dot(pick, x_ref[...], preferred_element_type=f32)
    rows_dy = jnp.dot(gated, dy_ref[...], preferred_element_type=f32)
    for j in range(width):
        cols = slice(j * LANES, (j + 1) * LANES)
        wide_ref[pl.ds(j, slots, stride=2 * width), :] = rows_x[:, cols]
        wide_ref[pl.ds(width + j, slots, stride=2 * width), :] = rows_dy[:, cols]
    out_ref[...] = wide_ref[...].astype(bf16)


def gelu_parts(pre):
    inner = jnp.tanh(gelu_scale * (pre + cubic_coef * pre * pre * pre))
    value = 0.5 * pre * (1.0 + inner)
    slope = 0.5 * (1.0 + inner) + 0.5 * pre * (1.0 - inner * inner) * gelu_scale * (
        1.0 + 3.0 * cubic_coef * pre * pre
    )
    return value, slope


def unpack_body(r0, r1, r2, r3, x_ref, dy_ref, wide_ref):
    slots, width = x_ref.shape
    tiles = width // LANES
    for i, ref in enumerate((r0, r1, r2, r3)):
        part = ref.shape[0]
        wide_ref[i * part : (i + 1) * part] = ref[...].astype(f32)
    for j in range(tiles):
        cols = slice(j * LANES, (j + 1) * LANES)
        x_ref[:, cols] = wide_ref[pl.ds(j, slots, stride=2 * tiles), :].astype(bf16)
        dy_ref[:, cols] = wide_ref[pl.ds(tiles + j, slots, stride=2 * tiles), :].astype(bf16)


def pair_of(w_ref, pair):
    return jnp.concatenate([w_ref[pair], w_ref[pair + 1]], axis=1)


def weight_gradient(units_ref, sides, grad_ref):
    slots = sides[0].shape[0]
    for pair in range(0, grad_ref.shape[0], 2):
        cols = slice(pair * LANES, (pair + 2) * LANES)
        grad = sum(
            lax.dot_general(
                units_ref[half * slots : (half + 1) * slots, cols],
                side,
                (((0,), (0,)), ((), ())),
                preferred_element_type=f32,
            )
            for half, side in enumerate(sides)
        ).astype(bf16)
        grad_ref[pair] = grad[:LANES]
        grad_ref[pair + 1] = grad[LANES:]


def first_body(xm_ref, xo_ref, dym_ref, dyo_ref, w_ref, act_ref, slope_ref, grad_ref):
    slots = xm_ref.shape[0]
    for half, x_ref in enumerate((xm_ref, xo_ref)):
        rows = slice(half * slots, (half + 1) * slots)
        for pair in range(0, w_ref.shape[0], 2):
            cols = slice(pair * LANES, (pair + 2) * LANES)
            pre = jnp.dot(x_ref[...], pair_of(w_ref, pair), preferred_element_type=f32)
            value, slope = gelu_parts(pre)
            act_ref[rows, cols] = value.astype(bf16)
            slope_ref[rows, cols] = slope
    weight_gradient(act_ref, (dym_ref[...], dyo_ref[...]), grad_ref)


def second_body(
    xm_ref, xo_ref, dym_ref, dyo_ref, act_ref, slope_ref, w_ref, dpre_ref, gate_ref, grad_ref
):
    slots = xm_ref.shape[0]
    for half, dy_ref in enumerate((dym_ref, dyo_ref)):
        rows = slice(half * slots, (half + 1) * slots)
        gates = []
        for pair in range(0, w_ref.shape[0], 2):
            cols = slice(pair * LANES, (pair + 2) * LANES)
            dy_proj = jnp.dot(dy_ref[...], pair_of(w_ref, pair), preferred_element_type=f32)
            dpre_ref[rows, cols] = (dy_proj * slope_ref[rows, cols]).astype(bf16)
            gate = act_ref[rows, cols].astype(f32) * dy_proj
            gates += [gate[:, :LANES], gate[:, LANES:]]
        gate_ref[rows] = sum(gates[1:], gates[0])
    weight_gradient(dpre_ref, (xm_ref[...], xo_ref[...]), grad_ref)


def dx_body(dpre_ref, w_ref, gate_ref, keep_ref, keep_gate_ref, give_ref):
    slots = keep_ref.shape[0]
    width = keep_ref.shape[1]
    weights = jnp.concatenate([w_ref[i] for i in range(w_ref.shape[0])], axis=1)
    dims = (((1,), (1,)), ((), ()))
    give = lax.dot_general(dpre_ref[slots:], weights, dims, preferred_element_type=f32)
    give_ref[:, :width] = give.astype(bf16)
    keep_ref[...] = lax.dot_general(dpre_ref[:slots], weights, dims, preferred_element_type=f32)
    gate = jnp.sum(gate_ref[:slots], axis=1, keepdims=True)
    keep_gate_ref[...] = jnp.broadcast_to(gate, keep_gate_ref.shape)
    gate = jnp.sum(gate_ref[slots:], axis=1, keepdims=True)
    coarse = gate.astype(bf16).astype(f32)
    fine = (gate - coarse).astype(bf16).astype(f32)
    lane = lax.broadcasted_iota(jnp.int32, (slots, LANES), 1)
    give_ref[:, width:] = jnp.where(
        lane == 0, coarse, jnp.where(lane == 1, fine, 0.0)
    ).astype(bf16)


def pack_body(experts, capacity, keep_ref, keep_gate_ref, took_ref, out_ref, rows_ref, wide_ref):
    slots = keep_ref.shape[0]
    width = keep_ref.shape[1]
    tiles = width // LANES
    step = (capacity + 1) * tiles
    for j in range(tiles):
        cols = slice(j * LANES, (j + 1) * LANES)
        total = keep_ref[:, cols] + took_ref[:, cols].astype(f32)
        rows_ref[j] = total.astype(bf16).astype(f32)
    gate = keep_gate_ref[:, 0:1] + jnp.sum(took_ref[:, width:].astype(f32), axis=1, keepdims=True)
    row = lax.broadcasted_iota(jnp.int32, (slots, LANES), 0)
    lane = lax.broadcasted_iota(jnp.int32, (slots, LANES), 1)
    spread = jnp.where(row % capacity == lane, gate, 0.0).astype(bf16)
    expert = lax.broadcasted_iota(jnp.int32, (experts, slots), 0)
    slot = lax.broadcasted_iota(jnp.int32, (experts, slots), 1)
    owner = (slot // capacity == expert).astype(f32).astype(bf16)
    table = jnp.dot(owner, spread, preferred_element_type=f32)
    for c in range(capacity):
        for j in range(tiles):
            wide_ref[pl.ds(c * tiles + j, experts, stride=step), :] = rows_ref[
                j, pl.ds(c, experts, stride=capacity), :
            ]
    for j in range(tiles):
        wide_ref[pl.ds(capacity * tiles + j, experts, stride=step), :] = (
            table if j == 0 else jnp.zeros_like(table)
        )
    places = out_ref.shape[0]
    planes = experts // places
    for i in range(planes):
        part = wide_ref[i * places * step : (i + 1) * places * step]
        out_ref[:, i * step : (i + 1) * step] = part.reshape(places, step, LANES).astype(bf16)


def combine_body(
    experts, capacity, plane_ref, ids_ref, gates_ref, b0, b1, b2, b3,
    dtok_ref, dgate_ref, wide_ref, rows_ref,
):
    slots = experts * capacity
    tiles = dtok_ref.shape[1] // LANES
    step = (capacity + 1) * tiles
    for i, ref in enumerate((b0, b1, b2, b3)):
        part = ref.shape[0]
        wide_ref[i * part : (i + 1) * part] = ref[...].astype(f32)
    for c in range(capacity):
        for j in range(tiles):
            rows_ref[j, pl.ds(c, experts, stride=capacity), :] = wide_ref[
                pl.ds(c * tiles + j, experts, stride=step), :
            ]
    table = wide_ref[pl.ds(capacity * tiles, experts, stride=step), :].astype(bf16)
    pick_first, pick_second = one_hots(ids_ref, plane_ref[0], experts, capacity, True)
    pick = (pick_first + pick_second).astype(bf16)
    for j in range(tiles):
        dtok_ref[:, j * LANES : (j + 1) * LANES] = lax.dot_general(
            pick, rows_ref[j].astype(bf16), (((0,), (0,)), ((), ())), preferred_element_type=f32
        ).astype(bf16)
    expert = lax.broadcasted_iota(jnp.int32, (slots, experts), 1)
    slot = lax.broadcasted_iota(jnp.int32, (slots, experts), 0)
    owner = (slot // capacity == expert).astype(f32).astype(bf16)
    by_slot = jnp.dot(owner, table, preferred_element_type=f32)
    row = lax.broadcasted_iota(jnp.int32, (slots, LANES), 0)
    lane = lax.broadcasted_iota(jnp.int32, (slots, LANES), 1)
    gate = jnp.sum(jnp.where(row % capacity == lane, by_slot, 0.0), axis=1, keepdims=True)
    gates = gates_ref[...].astype(f32)
    sums = jnp.concatenate(
        [
            jnp.sum(pick_first * gate, axis=0, keepdims=True),
            jnp.sum(pick_second * gate, axis=0, keepdims=True),
        ],
        axis=0,
    )
    dgate_ref[...] = (sums / gates).astype(bf16)


def finish_body(total_ref, out_ref):
    out_ref[...] = total_ref[...].astype(f32).T


def shards(tokens, out_grad, gates, expert_ids, w_in, w_out):
    tok_rows, width = tokens.shape
    experts = lax.axis_size("expert")
    replicas = lax.axis_size("dp")
    capacity = 3 * tok_rows // experts
    slots = experts * capacity
    tiles = width // LANES
    shard = w_in.shape[2]
    same_core = [[i for i in range(replicas) if i % 2 == c] for c in range(2)]
    swap = [(i, i ^ 1) for i in range(replicas)]
    sds = jax.ShapeDtypeStruct

    plane = ((lax.axis_index("expert") >> 2) & 3).astype(jnp.int32).reshape(1)
    in_plane = [[x * 16 + zl * 4 + y for x in range(4) for y in range(4)] for zl in range(4)]

    def device(z, core, x, y):
        return ((z >> 2) * 2 + core) * experts + x * 16 + (z & 3) * 4 + y

    def along_z(hops):
        length = 2 * replicas
        return [
            (device(z, c, x, y), device((z + hops(z)) % length, c, x, y))
            for z in range(length) for c in range(2) for x in range(4) for y in range(4)
        ]

    out_perms = [along_z(lambda z: 1), along_z(lambda z: -2 if z % 2 else 2), along_z(lambda z: -1)]
    home_perms = [[(b, a) for a, b in perm] for perm in out_perms]

    def move(values, perms):
        return values[:1] + [
            lax.ppermute(v, ("dp", "expert"), perm) for v, perm in zip(values[1:], perms)
        ]

    def by_plane(array, rows):
        return [
            array[:, i * rows : (i + 1) * rows].reshape(experts // 4 * rows, LANES)
            for i in range(4)
        ]

    def send(value, perm):
        return lax.ppermute(value, "dp", perm)

    wi = w_in.reshape(width, shard)
    wo = w_out.reshape(width, shard)
    ids = expert_ids.T
    gates_row = gates.T

    def gather(w):
        return lax.all_gather(w, "dp", axis=0, tiled=False, axis_index_groups=same_core)

    def reduce(grads):
        return lax.psum_scatter(
            grads, "dp", scatter_dimension=0, tiled=False, axis_index_groups=same_core
        )

    full_in = gather(wi)
    chunk = capacity * 2 * tiles
    wide = pltpu.VMEM((slots * 2 * tiles, LANES), f32)
    payload = call(
        lambda *refs: dispatch_body(experts, capacity, *refs),
        sds((slots * 2 * tiles, LANES), bf16),
        "dispatch",
        [wide],
        1,
        4,
    )(plane, ids, gates_row, tokens, out_grad)
    got = lax.all_to_all(
        payload.reshape(experts // 4, 4 * chunk, LANES),
        "expert", split_axis=0, concat_axis=0, tiled=True, axis_index_groups=in_plane,
    )
    got, full_in = lax.optimization_barrier((got, full_in))
    got = move(by_plane(got, chunk), out_perms)
    got, wo = lax.optimization_barrier((got, wo))
    full_out = gather(wo)
    rows = sds((slots, width), bf16)
    x, dy = call(unpack_body, (rows, rows), "unpack", [wide])(*got)
    sides = (x, send(x, swap), dy, send(dy, swap))
    blocks = replicas // 2
    hidden = (2 * slots, blocks * shard)
    grad = sds((blocks, shard, width), bf16)
    act, slope, grads_out = call(
        first_body, (sds(hidden, bf16), sds(hidden, f32), grad), "first"
    )(*sides, full_in)
    total_out = reduce(grads_out)
    d_pre, gate, grads_in = call(
        second_body, (sds(hidden, bf16), sds((2 * slots, LANES), f32), grad), "second"
    )(*sides, act, slope, full_out)
    total_in = reduce(grads_in)
    keep, keep_gate, give = call(
        dx_body,
        (sds((slots, width), f32), sds((slots, LANES), f32), sds((slots, width + LANES), bf16)),
        "input_gradient",
    )(d_pre, full_in, gate)
    took = send(give, swap)
    back = call(
        lambda *refs: pack_body(experts, capacity, *refs),
        sds((experts // 4, 4 * (capacity + 1) * tiles, LANES), bf16),
        "pack",
        [
            pltpu.VMEM((tiles, slots, LANES), f32),
            pltpu.VMEM((experts * (capacity + 1) * tiles, LANES), f32),
        ],
    )(keep, keep_gate, took)
    chunk = (capacity + 1) * tiles
    back = lax.all_to_all(
        back,
        "expert", split_axis=0, concat_axis=0, tiled=True, axis_index_groups=in_plane,
    )
    back = move(by_plane(back, chunk), home_perms)
    d_tokens, gate_grad = call(
        lambda *refs: combine_body(experts, capacity, *refs),
        (sds((tok_rows, width), bf16), sds((2, tok_rows), bf16)),
        "combine",
        [
            pltpu.VMEM((experts * (capacity + 1) * tiles, LANES), f32),
            pltpu.VMEM((tiles, slots, LANES), f32),
        ],
        1,
        6,
    )(plane, ids, gates_row, *back)
    d_tokens, gate_grad, total_in = lax.optimization_barrier((d_tokens, gate_grad, total_in))
    own = sds((width, shard), f32)
    grad_in = call(finish_body, own, "finish_in")(total_in)
    grad_out = call(finish_body, own, "finish_out")(total_out)
    return d_tokens, gate_grad.T, grad_in[None], grad_out[None]


def solution(mesh):
    by_token = P(("dp", "expert"), None)
    by_expert = P("expert", None, "dp")
    return jax.shard_map(
        shards,
        mesh=mesh,
        in_specs=(by_token, by_token, by_token, by_token, by_expert, by_expert),
        out_specs=(by_token, by_token, by_expert, by_expert),
        check_vma=False,
    )
```

```python
import jax
import jax.numpy as jnp
from jax import lax
from jax.experimental import pallas as pl
from jax.experimental.pallas import tpu as pltpu
from jax.sharding import PartitionSpec as P

gelu_scale = 0.7978845608028654
cubic_coef = 0.044715
bf16 = jnp.bfloat16
f32 = jnp.float32
LANES = 128
VMEM_BYTES = 56 << 20


def call(body, out_shape, name, scratch=(), scalars=0, arrays=0, **specs):
    if scalars:
        specs["in_specs"] = [pl.BlockSpec(memory_space=pltpu.SMEM)] * scalars + [
            pl.BlockSpec(memory_space=pltpu.VMEM)
        ] * arrays
    return pl.pallas_call(
        body,
        out_shape=out_shape,
        **specs,
        scratch_shapes=scratch,
        name=name,
        compiler_params=pltpu.CompilerParams(vmem_limit_bytes=VMEM_BYTES),
    )


def slot_targets(ids_ref, plane, experts, capacity, planes_first):
    tokens = ids_ref.shape[1]

    def near_order(expert):
        up = (((expert >> 2) & 3) - plane) & 3
        place = (expert >> 4) * 4 + (expert & 3)
        return up * 16 + place if planes_first else place * 4 + up

    first = near_order(ids_ref[0:1, :])
    second = near_order(ids_ref[1:2, :])
    expert = lax.broadcasted_iota(jnp.int32, (experts, tokens), 0)
    is_first = (expert == first).astype(f32)
    is_second = (expert == second).astype(f32)
    before = (
        lax.broadcasted_iota(jnp.int32, (tokens, tokens), 0)
        < lax.broadcasted_iota(jnp.int32, (tokens, tokens), 1)
    ).astype(f32)
    earlier = jnp.dot(
        (is_first + is_second).astype(bf16), before.astype(bf16), preferred_element_type=f32
    )
    slot_first = jnp.sum(earlier * is_first, axis=0, keepdims=True).astype(jnp.int32)
    slot_second = jnp.sum(earlier * is_second, axis=0, keepdims=True).astype(jnp.int32)
    return first * capacity + slot_first, second * capacity + slot_second


def one_hots(ids_ref, plane, experts, capacity, planes_first):
    tokens = ids_ref.shape[1]
    first, second = slot_targets(ids_ref, plane, experts, capacity, planes_first)
    slot = lax.broadcasted_iota(jnp.int32, (experts * capacity, tokens), 0)
    return (slot == first).astype(f32), (slot == second).astype(f32)


def dispatch_body(experts, capacity, plane_ref, ids_ref, gates_ref, x_ref, dy_ref, out_ref, wide_ref):
    width = x_ref.shape[1] // LANES
    slots = experts * capacity
    pick_first, pick_second = one_hots(ids_ref, plane_ref[0], experts, capacity, False)
    gates = gates_ref[...].astype(f32)
    pick = (pick_first + pick_second).astype(bf16)
    gated = (pick_first * gates[0:1, :] + pick_second * gates[1:2, :]).astype(bf16)
    rows_x = jnp.dot(pick, x_ref[...], preferred_element_type=f32)
    rows_dy = jnp.dot(gated, dy_ref[...], preferred_element_type=f32)
    for j in range(width):
        cols = slice(j * LANES, (j + 1) * LANES)
        wide_ref[pl.ds(j, slots, stride=2 * width), :] = rows_x[:, cols]
        wide_ref[pl.ds(width + j, slots, stride=2 * width), :] = rows_dy[:, cols]
    out_ref[...] = wide_ref[...].astype(bf16)


def gelu_parts(pre):
    inner = jnp.tanh(gelu_scale * (pre + cubic_coef * pre * pre * pre))
    value = 0.5 * pre * (1.0 + inner)
    slope = 0.5 * (1.0 + inner) + 0.5 * pre * (1.0 - inner * inner) * gelu_scale * (
        1.0 + 3.0 * cubic_coef * pre * pre
    )
    return value, slope


def unpack_body(capacity, got_ref, r0, r1, r2, r3, wide_ref):
    slots, width = r0.shape
    places = slots // capacity
    tiles = width // LANES
    step = 4 * capacity * tiles
    wide_ref[...] = got_ref[...].astype(f32)
    for i, ref in enumerate((r0, r1, r2, r3)):
        for c in range(capacity):
            for j in range(tiles):
                start = (i * capacity + c) * tiles + j
                ref[c * places : (c + 1) * places, j * LANES : (j + 1) * LANES] = wide_ref[
                    pl.ds(start, places, stride=step), :
                ].astype(bf16)


def project(rows_ref, w_ref, dpre_ref, act_ref, gate_ref):
    width = rows_ref.shape[1] // 2
    w_first = jnp.concatenate([w_ref[0, :width], w_ref[1, :width]], axis=1)
    w_second = jnp.concatenate([w_ref[0, width:], w_ref[1, width:]], axis=1)
    pre = jnp.dot(rows_ref[:, :width], w_first, preferred_element_type=f32)
    dy_proj = jnp.dot(rows_ref[:, width:], w_second, preferred_element_type=f32)
    value, slope = gelu_parts(pre)
    activated = value.astype(bf16)
    gate = activated.astype(f32) * dy_proj
    dpre_ref[...] = (dy_proj * slope).astype(bf16)
    act_ref[...] = activated
    lanes = gate[:, :LANES] + gate[:, LANES:]

    @pl.when(pl.program_id(0) == 0)
    def _():
        gate_ref[...] = lanes

    @pl.when(pl.program_id(0) > 0)
    def _():
        gate_ref[...] += lanes


def other_body(
    mine_ref, other_ref, dpre_in_ref, act_in_ref, w_ref, dpre_ref, gate_ref, grad_ref, act_ref
):
    width = mine_ref.shape[1] // 2
    project(other_ref, w_ref, dpre_ref, act_ref, gate_ref)
    dims = (((0,), (0,)), ((), ()))
    for row, ours, theirs, cols in (
        (0, dpre_in_ref, dpre_ref, slice(0, width)),
        (LANES, act_in_ref, act_ref, slice(width, 2 * width)),
    ):
        grad = lax.dot_general(ours[...], mine_ref[:, cols], dims, preferred_element_type=f32)
        grad += lax.dot_general(theirs[...], other_ref[:, cols], dims, preferred_element_type=f32)
        grad = grad.astype(bf16)
        grad_ref[0, row : row + LANES] = grad[:LANES]
        grad_ref[1, row : row + LANES] = grad[LANES:]


def dx_body(dpre_m, dpre_o, w_ref, gate_m, gate_o, keep_ref, keep_gate_ref, give_ref):
    slots = keep_ref.shape[0]
    width = keep_ref.shape[1]
    weights = jnp.concatenate([w_ref[i, :width] for i in range(w_ref.shape[0])], axis=1)
    dims = (((1,), (1,)), ((), ()))
    give = lax.dot_general(dpre_o[...], weights, dims, preferred_element_type=f32)
    give_ref[:, :width] = give.astype(bf16)
    keep_ref[...] = lax.dot_general(dpre_m[...], weights, dims, preferred_element_type=f32)
    gate = jnp.sum(gate_m[...], axis=1, keepdims=True)
    keep_gate_ref[...] = jnp.broadcast_to(gate, keep_gate_ref.shape)
    gate = jnp.sum(gate_o[...], axis=1, keepdims=True)
    coarse = gate.astype(bf16).astype(f32)
    fine = (gate - coarse).astype(bf16).astype(f32)
    lane = lax.broadcasted_iota(jnp.int32, (slots, LANES), 1)
    give_ref[:, width:] = jnp.where(
        lane == 0, coarse, jnp.where(lane == 1, fine, 0.0)
    ).astype(bf16)


def pack_body(experts, capacity, keep_ref, keep_gate_ref, took_ref, out_ref, rows_ref, wide_ref):
    slots = keep_ref.shape[0]
    width = keep_ref.shape[1]
    tiles = width // LANES
    step = (capacity + 1) * tiles
    for j in range(tiles):
        cols = slice(j * LANES, (j + 1) * LANES)
        total = keep_ref[:, cols] + took_ref[:, cols].astype(f32)
        rows_ref[j] = total.astype(bf16).astype(f32)
    gate = keep_gate_ref[:, 0:1] + jnp.sum(took_ref[:, width:].astype(f32), axis=1, keepdims=True)
    places = out_ref.shape[0]
    planes = experts // places
    row = lax.broadcasted_iota(jnp.int32, (slots, LANES), 0)
    lane = lax.broadcasted_iota(jnp.int32, (slots, LANES), 1)
    spread = jnp.where((row // places) % capacity == lane, gate, 0.0).astype(bf16)
    block = lax.broadcasted_iota(jnp.int32, (experts, slots), 0)
    slot = lax.broadcasted_iota(jnp.int32, (experts, slots), 1)
    owner = (slot % places * planes + slot // (capacity * places) == block).astype(f32)
    table = jnp.dot(owner.astype(bf16), spread, preferred_element_type=f32)
    for i in range(planes):
        for c in range(capacity):
            first = (i * capacity + c) * places
            for j in range(tiles):
                wide_ref[pl.ds(i * step + c * tiles + j, places, stride=planes * step), :] = (
                    rows_ref[j, first : first + places, :]
                )
    for j in range(tiles):
        wide_ref[pl.ds(capacity * tiles + j, experts, stride=step), :] = (
            table if j == 0 else jnp.zeros_like(table)
        )
    out_ref[...] = wide_ref[...].reshape(out_ref.shape).astype(bf16)


def combine_body(
    experts, capacity, plane_ref, ids_ref, gates_ref, b0, b1, b2, b3,
    dtok_ref, dgate_ref, wide_ref, rows_ref,
):
    slots = experts * capacity
    tiles = dtok_ref.shape[1] // LANES
    step = (capacity + 1) * tiles
    for i, ref in enumerate((b0, b1, b2, b3)):
        part = ref.shape[0]
        wide_ref[i * part : (i + 1) * part] = ref[...].astype(f32)
    for c in range(capacity):
        for j in range(tiles):
            rows_ref[j, pl.ds(c, experts, stride=capacity), :] = wide_ref[
                pl.ds(c * tiles + j, experts, stride=step), :
            ]
    table = wide_ref[pl.ds(capacity * tiles, experts, stride=step), :].astype(bf16)
    pick_first, pick_second = one_hots(ids_ref, plane_ref[0], experts, capacity, True)
    pick = (pick_first + pick_second).astype(bf16)
    for j in range(tiles):
        dtok_ref[:, j * LANES : (j + 1) * LANES] = lax.dot_general(
            pick, rows_ref[j].astype(bf16), (((0,), (0,)), ((), ())), preferred_element_type=f32
        ).astype(bf16)
    expert = lax.broadcasted_iota(jnp.int32, (slots, experts), 1)
    slot = lax.broadcasted_iota(jnp.int32, (slots, experts), 0)
    owner = (slot // capacity == expert).astype(f32).astype(bf16)
    by_slot = jnp.dot(owner, table, preferred_element_type=f32)
    row = lax.broadcasted_iota(jnp.int32, (slots, LANES), 0)
    lane = lax.broadcasted_iota(jnp.int32, (slots, LANES), 1)
    gate = jnp.sum(jnp.where(row % capacity == lane, by_slot, 0.0), axis=1, keepdims=True)
    gates = gates_ref[...].astype(f32)
    sums = jnp.concatenate(
        [
            jnp.sum(pick_first * gate, axis=0, keepdims=True),
            jnp.sum(pick_second * gate, axis=0, keepdims=True),
        ],
        axis=0,
    )
    dgate_ref[...] = (sums / gates).astype(bf16)


def finish_body(total_ref, gi_ref, go_ref):
    total = total_ref[...].astype(f32)
    gi_ref[...] = total[:LANES].T
    go_ref[...] = total[LANES:].T


def shards(tokens, out_grad, gates, expert_ids, w_in, w_out):
    tok_rows, width = tokens.shape
    experts = lax.axis_size("expert")
    replicas = lax.axis_size("dp")
    capacity = 3 * tok_rows // experts
    slots = experts * capacity
    tiles = width // LANES
    shard = w_in.shape[2]
    same_core = [[i for i in range(replicas) if i % 2 == c] for c in range(2)]
    swap = [(i, i ^ 1) for i in range(replicas)]
    sds = jax.ShapeDtypeStruct

    plane = ((lax.axis_index("expert") >> 2) & 3).astype(jnp.int32).reshape(1)
    in_plane = [[x * 16 + zl * 4 + y for x in range(4) for y in range(4)] for zl in range(4)]

    def device(z, core, x, y):
        return ((z >> 2) * 2 + core) * experts + x * 16 + (z & 3) * 4 + y

    def along_z(hops):
        length = 2 * replicas
        return [
            (device(z, c, x, y), device((z + hops(z)) % length, c, x, y))
            for z in range(length) for c in range(2) for x in range(4) for y in range(4)
        ]

    out_perms = [along_z(lambda z: 1), along_z(lambda z: -2 if z % 2 else 2), along_z(lambda z: -1)]
    home_perms = [[(b, a) for a, b in perm] for perm in out_perms]

    def move(values, perms):
        return values[:1] + [
            lax.ppermute(v, ("dp", "expert"), perm) for v, perm in zip(values[1:], perms)
        ]

    def by_plane(array, rows):
        return [
            array[:, i * rows : (i + 1) * rows].reshape(experts // 4 * rows, LANES)
            for i in range(4)
        ]

    def send(value, perm):
        return lax.ppermute(value, "dp", perm)

    wi = w_in.reshape(width, shard)
    wo = w_out.reshape(width, shard)
    ids = expert_ids.T
    gates_row = gates.T

    weights = lax.all_gather(
        jnp.concatenate([wi, wo], axis=0), "dp", axis=0, tiled=False, axis_index_groups=same_core
    )

    chunk = capacity * 2 * tiles
    wide = pltpu.VMEM((slots * 2 * tiles, LANES), f32)
    payload = call(
        lambda *refs: dispatch_body(experts, capacity, *refs),
        sds((slots * 2 * tiles, LANES), bf16),
        "dispatch",
        [wide],
        1,
        4,
    )(plane, ids, gates_row, tokens, out_grad)
    got = lax.all_to_all(
        payload.reshape(experts // 4, 4 * chunk, LANES),
        "expert", split_axis=0, concat_axis=0, tiled=True, axis_index_groups=in_plane,
    )
    got = call(
        lambda *refs: unpack_body(capacity, *refs),
        (sds((slots // 4, 2 * width), bf16),) * 4,
        "unpack",
        [wide],
    )(got.reshape(slots * 2 * tiles, LANES))
    mine = jnp.concatenate(move(list(got), out_perms), axis=0)
    mine, weights = lax.optimization_barrier((mine, weights))
    other = send(mine, swap)
    blocks = replicas // 2
    hidden = sds((slots, blocks * shard), bf16)
    gate_shape = sds((slots, LANES), f32)

    def whole(shape):
        return pl.BlockSpec(shape, lambda i: (0,) * len(shape))

    all_rows = whole((slots, 2 * width))
    all_gates = whole((slots, LANES))
    some_units = pl.BlockSpec((slots, 2 * shard), lambda i: (0, i))
    some_weights = pl.BlockSpec((2, 2 * width, shard), lambda i: (i, 0, 0))
    dpre_mine, act_mine, gate_mine = call(
        project,
        (hidden, hidden, gate_shape),
        "mine",
        grid=(blocks // 2,),
        in_specs=[all_rows, some_weights],
        out_specs=(some_units, some_units, all_gates),
    )(mine, weights)
    dpre_other, gate_other, grads = call(
        other_body,
        (hidden, gate_shape, sds((blocks, 2 * shard, width), bf16)),
        "other",
        [pltpu.VMEM((slots, 2 * shard), bf16)],
        grid=(blocks // 2,),
        in_specs=[all_rows, all_rows, some_units, some_units, some_weights],
        out_specs=(some_units, all_gates, pl.BlockSpec((2, 2 * shard, width), lambda i: (i, 0, 0))),
    )(mine, other, dpre_mine, act_mine, weights)
    total = lax.psum_scatter(
        grads, "dp", scatter_dimension=0, tiled=False, axis_index_groups=same_core
    )
    keep, keep_gate, give = call(
        dx_body,
        (sds((slots, width), f32), sds((slots, LANES), f32), sds((slots, width + LANES), bf16)),
        "input_gradient",
    )(dpre_mine, dpre_other, weights, gate_mine, gate_other)
    took = send(give, swap)
    back = call(
        lambda *refs: pack_body(experts, capacity, *refs),
        sds((experts // 4, 4 * (capacity + 1) * tiles, LANES), bf16),
        "pack",
        [
            pltpu.VMEM((tiles, slots, LANES), f32),
            pltpu.VMEM((experts * (capacity + 1) * tiles, LANES), f32),
        ],
    )(keep, keep_gate, took)
    chunk = (capacity + 1) * tiles
    back = lax.all_to_all(
        back,
        "expert", split_axis=0, concat_axis=0, tiled=True, axis_index_groups=in_plane,
    )
    back = move(by_plane(back, chunk), home_perms)
    d_tokens, gate_grad = call(
        lambda *refs: combine_body(experts, capacity, *refs),
        (sds((tok_rows, width), bf16), sds((2, tok_rows), bf16)),
        "combine",
        [
            pltpu.VMEM((experts * (capacity + 1) * tiles, LANES), f32),
            pltpu.VMEM((tiles, slots, LANES), f32),
        ],
        1,
        6,
    )(plane, ids, gates_row, *back)
    d_tokens, gate_grad, total = lax.optimization_barrier((d_tokens, gate_grad, total))
    own = sds((width, shard), f32)
    grad_in, grad_out = call(finish_body, (own, own), "finish")(total)
    return d_tokens, gate_grad.T, grad_in[None], grad_out[None]


def solution(mesh):
    by_token = P(("dp", "expert"), None)
    by_expert = P("expert", None, "dp")
    return jax.shard_map(
        shards,
        mesh=mesh,
        in_specs=(by_token, by_token, by_token, by_token, by_expert, by_expert),
        out_specs=(by_token, by_token, by_expert, by_expert),
        check_vma=False,
    )
```

```python
import jax
import jax.numpy as jnp
from jax import lax
from jax.experimental import pallas as pl
from jax.experimental.pallas import tpu as pltpu
from jax.sharding import PartitionSpec as P

gelu_scale = 0.7978845608028654
cubic_coef = 0.044715
bf16 = jnp.bfloat16
f32 = jnp.float32
LANES = 128
VMEM_BYTES = 56 << 20


def call(body, out_shape, name, scratch=(), scalars=0, arrays=0, **specs):
    if scalars:
        specs["in_specs"] = [pl.BlockSpec(memory_space=pltpu.SMEM)] * scalars + [
            pl.BlockSpec(memory_space=pltpu.VMEM)
        ] * arrays
    return pl.pallas_call(
        body,
        out_shape=out_shape,
        **specs,
        scratch_shapes=scratch,
        name=name,
        compiler_params=pltpu.CompilerParams(vmem_limit_bytes=VMEM_BYTES),
    )


def slot_targets(ids_ref, plane, experts, capacity, planes_first):
    tokens = ids_ref.shape[1]

    def near_order(expert):
        up = (((expert >> 2) & 3) - plane) & 3
        place = (expert >> 4) * 4 + (expert & 3)
        return up * 16 + place if planes_first else place * 4 + up

    first = near_order(ids_ref[0:1, :])
    second = near_order(ids_ref[1:2, :])
    expert = lax.broadcasted_iota(jnp.int32, (experts, tokens), 0)
    is_first = (expert == first).astype(f32)
    is_second = (expert == second).astype(f32)
    before = (
        lax.broadcasted_iota(jnp.int32, (tokens, tokens), 0)
        < lax.broadcasted_iota(jnp.int32, (tokens, tokens), 1)
    ).astype(f32)
    earlier = jnp.dot(
        (is_first + is_second).astype(bf16), before.astype(bf16), preferred_element_type=f32
    )
    slot_first = jnp.sum(earlier * is_first, axis=0, keepdims=True).astype(jnp.int32)
    slot_second = jnp.sum(earlier * is_second, axis=0, keepdims=True).astype(jnp.int32)
    return first * capacity + slot_first, second * capacity + slot_second


def one_hots(ids_ref, plane, experts, capacity, planes_first):
    tokens = ids_ref.shape[1]
    first, second = slot_targets(ids_ref, plane, experts, capacity, planes_first)
    slot = lax.broadcasted_iota(jnp.int32, (experts * capacity, tokens), 0)
    return (slot == first).astype(f32), (slot == second).astype(f32)


def dispatch_body(experts, capacity, plane_ref, ids_ref, gates_ref, x_ref, dy_ref, out_ref, wide_ref):
    width = x_ref.shape[1] // LANES
    slots = experts * capacity
    pick_first, pick_second = one_hots(ids_ref, plane_ref[0], experts, capacity, False)
    gates = gates_ref[...].astype(f32)
    pick = (pick_first + pick_second).astype(bf16)
    gated = (pick_first * gates[0:1, :] + pick_second * gates[1:2, :]).astype(bf16)
    rows_x = jnp.dot(pick, x_ref[...], preferred_element_type=f32)
    rows_dy = jnp.dot(gated, dy_ref[...], preferred_element_type=f32)
    for j in range(width):
        cols = slice(j * LANES, (j + 1) * LANES)
        wide_ref[pl.ds(j, slots, stride=2 * width), :] = rows_x[:, cols]
        wide_ref[pl.ds(width + j, slots, stride=2 * width), :] = rows_dy[:, cols]
    out_ref[...] = wide_ref[...].astype(bf16)


def gelu_parts(pre):
    inner = jnp.tanh(gelu_scale * (pre + cubic_coef * pre * pre * pre))
    value = 0.5 * pre * (1.0 + inner)
    slope = 0.5 * (1.0 + inner) + 0.5 * pre * (1.0 - inner * inner) * gelu_scale * (
        1.0 + 3.0 * cubic_coef * pre * pre
    )
    return value, slope


def unpack_body(capacity, got_ref, r0, r1, r2, r3, wide_ref):
    slots, width = r0.shape
    places = slots // capacity
    tiles = width // LANES
    step = 4 * capacity * tiles
    wide_ref[...] = got_ref[...].astype(f32)
    for i, ref in enumerate((r0, r1, r2, r3)):
        for c in range(capacity):
            for j in range(tiles):
                start = (i * capacity + c) * tiles + j
                ref[c * places : (c + 1) * places, j * LANES : (j + 1) * LANES] = wide_ref[
                    pl.ds(start, places, stride=step), :
                ].astype(bf16)


def project(rows_ref, w_ref, dpre_ref, act_ref, gate_ref):
    width = rows_ref.shape[1] // 2
    w_first = jnp.concatenate([w_ref[0, :width], w_ref[1, :width]], axis=1)
    w_second = jnp.concatenate([w_ref[0, width:], w_ref[1, width:]], axis=1)
    first_step = pl.program_id(0) == 0
    chunk = rows_ref.shape[0] // 3
    for start in range(0, rows_ref.shape[0], chunk):
        rows = slice(start, start + chunk)
        pre = jnp.dot(rows_ref[rows, :width], w_first, preferred_element_type=f32)
        dy_proj = jnp.dot(rows_ref[rows, width:], w_second, preferred_element_type=f32)
        value, slope = gelu_parts(pre)
        activated = value.astype(bf16)
        gate = activated.astype(f32) * dy_proj
        dpre_ref[rows] = (dy_proj * slope).astype(bf16)
        act_ref[rows] = activated
        before = jnp.where(first_step, 0.0, gate_ref[rows])
        gate_ref[rows] = before + gate[:, :LANES] + gate[:, LANES:]


def other_body(
    mine_ref, other_ref, dpre_in_ref, act_in_ref, w_ref, dpre_ref, gate_ref, grad_ref, act_ref
):
    width = mine_ref.shape[1] // 2
    project(other_ref, w_ref, dpre_ref, act_ref, gate_ref)
    dims = (((0,), (0,)), ((), ()))
    for row, ours, theirs, cols in (
        (0, dpre_in_ref, dpre_ref, slice(0, width)),
        (LANES, act_in_ref, act_ref, slice(width, 2 * width)),
    ):
        grad = lax.dot_general(ours[...], mine_ref[:, cols], dims, preferred_element_type=f32)
        grad += lax.dot_general(theirs[...], other_ref[:, cols], dims, preferred_element_type=f32)
        grad = grad.astype(bf16)
        grad_ref[0, row : row + LANES] = grad[:LANES]
        grad_ref[1, row : row + LANES] = grad[LANES:]


def dx_body(dpre_m, dpre_o, w_ref, gate_m, gate_o, keep_ref, keep_gate_ref, give_ref):
    slots = keep_ref.shape[0]
    width = keep_ref.shape[1]
    weights = jnp.concatenate([w_ref[i, :width] for i in range(w_ref.shape[0])], axis=1)
    dims = (((1,), (1,)), ((), ()))
    give = lax.dot_general(dpre_o[...], weights, dims, preferred_element_type=f32)
    give_ref[:, :width] = give.astype(bf16)
    keep_ref[...] = lax.dot_general(dpre_m[...], weights, dims, preferred_element_type=f32)
    gate = jnp.sum(gate_m[...], axis=1, keepdims=True)
    keep_gate_ref[...] = jnp.broadcast_to(gate, keep_gate_ref.shape)
    gate = jnp.sum(gate_o[...], axis=1, keepdims=True)
    coarse = gate.astype(bf16).astype(f32)
    fine = (gate - coarse).astype(bf16).astype(f32)
    lane = lax.broadcasted_iota(jnp.int32, (slots, LANES), 1)
    give_ref[:, width:] = jnp.where(
        lane == 0, coarse, jnp.where(lane == 1, fine, 0.0)
    ).astype(bf16)


def pack_body(experts, capacity, keep_ref, keep_gate_ref, took_ref, out_ref, rows_ref, wide_ref):
    slots = keep_ref.shape[0]
    width = keep_ref.shape[1]
    tiles = width // LANES
    step = (capacity + 1) * tiles
    for j in range(tiles):
        cols = slice(j * LANES, (j + 1) * LANES)
        total = keep_ref[:, cols] + took_ref[:, cols].astype(f32)
        rows_ref[j] = total.astype(bf16).astype(f32)
    gate = keep_gate_ref[:, 0:1] + jnp.sum(took_ref[:, width:].astype(f32), axis=1, keepdims=True)
    places = out_ref.shape[0]
    planes = experts // places
    row = lax.broadcasted_iota(jnp.int32, (slots, LANES), 0)
    lane = lax.broadcasted_iota(jnp.int32, (slots, LANES), 1)
    spread = jnp.where((row // places) % capacity == lane, gate, 0.0).astype(bf16)
    block = lax.broadcasted_iota(jnp.int32, (experts, slots), 0)
    slot = lax.broadcasted_iota(jnp.int32, (experts, slots), 1)
    owner = (slot % places * planes + slot // (capacity * places) == block).astype(f32)
    table = jnp.dot(owner.astype(bf16), spread, preferred_element_type=f32)
    for i in range(planes):
        for c in range(capacity):
            first = (i * capacity + c) * places
            for j in range(tiles):
                wide_ref[pl.ds(i * step + c * tiles + j, places, stride=planes * step), :] = (
                    rows_ref[j, first : first + places, :]
                )
    for j in range(tiles):
        wide_ref[pl.ds(capacity * tiles + j, experts, stride=step), :] = (
            table if j == 0 else jnp.zeros_like(table)
        )
    out_ref[...] = wide_ref[...].reshape(out_ref.shape).astype(bf16)


def combine_body(
    experts, capacity, plane_ref, ids_ref, gates_ref, b0, b1, b2, b3,
    dtok_ref, dgate_ref, wide_ref, rows_ref,
):
    slots = experts * capacity
    tiles = dtok_ref.shape[1] // LANES
    step = (capacity + 1) * tiles
    for i, ref in enumerate((b0, b1, b2, b3)):
        part = ref.shape[0]
        wide_ref[i * part : (i + 1) * part] = ref[...].astype(f32)
    for c in range(capacity):
        for j in range(tiles):
            rows_ref[j, pl.ds(c, experts, stride=capacity), :] = wide_ref[
                pl.ds(c * tiles + j, experts, stride=step), :
            ]
    table = wide_ref[pl.ds(capacity * tiles, experts, stride=step), :].astype(bf16)
    pick_first, pick_second = one_hots(ids_ref, plane_ref[0], experts, capacity, True)
    pick = (pick_first + pick_second).astype(bf16)
    for j in range(tiles):
        dtok_ref[:, j * LANES : (j + 1) * LANES] = lax.dot_general(
            pick, rows_ref[j].astype(bf16), (((0,), (0,)), ((), ())), preferred_element_type=f32
        ).astype(bf16)
    expert = lax.broadcasted_iota(jnp.int32, (slots, experts), 1)
    slot = lax.broadcasted_iota(jnp.int32, (slots, experts), 0)
    owner = (slot // capacity == expert).astype(f32).astype(bf16)
    by_slot = jnp.dot(owner, table, preferred_element_type=f32)
    row = lax.broadcasted_iota(jnp.int32, (slots, LANES), 0)
    lane = lax.broadcasted_iota(jnp.int32, (slots, LANES), 1)
    gate = jnp.sum(jnp.where(row % capacity == lane, by_slot, 0.0), axis=1, keepdims=True)
    gates = gates_ref[...].astype(f32)
    sums = jnp.concatenate(
        [
            jnp.sum(pick_first * gate, axis=0, keepdims=True),
            jnp.sum(pick_second * gate, axis=0, keepdims=True),
        ],
        axis=0,
    )
    dgate_ref[...] = (sums / gates).astype(bf16)


def finish_body(total_ref, gi_ref, go_ref):
    total = total_ref[...].astype(f32)
    gi_ref[...] = total[:LANES].T
    go_ref[...] = total[LANES:].T


def shards(tokens, out_grad, gates, expert_ids, w_in, w_out):
    tok_rows, width = tokens.shape
    experts = lax.axis_size("expert")
    replicas = lax.axis_size("dp")
    capacity = 3 * tok_rows // experts
    slots = experts * capacity
    tiles = width // LANES
    shard = w_in.shape[2]
    same_core = [[i for i in range(replicas) if i % 2 == c] for c in range(2)]
    swap = [(i, i ^ 1) for i in range(replicas)]
    sds = jax.ShapeDtypeStruct

    plane = ((lax.axis_index("expert") >> 2) & 3).astype(jnp.int32).reshape(1)
    in_plane = [[x * 16 + zl * 4 + y for x in range(4) for y in range(4)] for zl in range(4)]

    def device(z, core, x, y):
        return ((z >> 2) * 2 + core) * experts + x * 16 + (z & 3) * 4 + y

    def along_z(hops):
        length = 2 * replicas
        return [
            (device(z, c, x, y), device((z + hops(z)) % length, c, x, y))
            for z in range(length) for c in range(2) for x in range(4) for y in range(4)
        ]

    out_perms = [along_z(lambda z: 1), along_z(lambda z: -2 if z % 2 else 2), along_z(lambda z: -1)]
    home_perms = [[(b, a) for a, b in perm] for perm in out_perms]

    def move(values, perms):
        return values[:1] + [
            lax.ppermute(v, ("dp", "expert"), perm) for v, perm in zip(values[1:], perms)
        ]

    def by_plane(array, rows):
        return [
            array[:, i * rows : (i + 1) * rows].reshape(experts // 4 * rows, LANES)
            for i in range(4)
        ]

    def send(value, perm):
        return lax.ppermute(value, "dp", perm)

    wi = w_in.reshape(width, shard)
    wo = w_out.reshape(width, shard)
    ids = expert_ids.T
    gates_row = gates.T

    weights = lax.all_gather(
        jnp.concatenate([wi, wo], axis=0), "dp", axis=0, tiled=False, axis_index_groups=same_core
    )

    chunk = capacity * 2 * tiles
    wide = pltpu.VMEM((slots * 2 * tiles, LANES), f32)
    payload = call(
        lambda *refs: dispatch_body(experts, capacity, *refs),
        sds((slots * 2 * tiles, LANES), bf16),
        "dispatch",
        [wide],
        1,
        4,
    )(plane, ids, gates_row, tokens, out_grad)
    got = lax.all_to_all(
        payload.reshape(experts // 4, 4 * chunk, LANES),
        "expert", split_axis=0, concat_axis=0, tiled=True, axis_index_groups=in_plane,
    )
    got = call(
        lambda *refs: unpack_body(capacity, *refs),
        (sds((slots // 4, 2 * width), bf16),) * 4,
        "unpack",
        [wide],
    )(got.reshape(slots * 2 * tiles, LANES))
    mine = jnp.concatenate(move(list(got), out_perms), axis=0)
    mine, weights = lax.optimization_barrier((mine, weights))
    other = send(mine, swap)
    blocks = replicas // 2
    hidden = sds((slots, blocks * shard), bf16)
    gate_shape = sds((slots, LANES), f32)

    def whole(shape):
        return pl.BlockSpec(shape, lambda i: (0,) * len(shape))

    all_rows = whole((slots, 2 * width))
    all_gates = whole((slots, LANES))
    some_units = pl.BlockSpec((slots, 2 * shard), lambda i: (0, i))
    some_weights = pl.BlockSpec((2, 2 * width, shard), lambda i: (i, 0, 0))
    dpre_mine, act_mine, gate_mine = call(
        project,
        (hidden, hidden, gate_shape),
        "mine",
        grid=(blocks // 2,),
        in_specs=[all_rows, some_weights],
        out_specs=(some_units, some_units, all_gates),
    )(mine, weights)
    dpre_other, gate_other, grads = call(
        other_body,
        (hidden, gate_shape, sds((blocks, 2 * shard, width), bf16)),
        "other",
        [pltpu.VMEM((slots, 2 * shard), bf16)],
        grid=(blocks // 2,),
        in_specs=[all_rows, all_rows, some_units, some_units, some_weights],
        out_specs=(some_units, all_gates, pl.BlockSpec((2, 2 * shard, width), lambda i: (i, 0, 0))),
    )(mine, other, dpre_mine, act_mine, weights)
    total = lax.psum_scatter(
        grads, "dp", scatter_dimension=0, tiled=False, axis_index_groups=same_core
    )
    keep, keep_gate, give = call(
        dx_body,
        (sds((slots, width), f32), sds((slots, LANES), f32), sds((slots, width + LANES), bf16)),
        "input_gradient",
    )(dpre_mine, dpre_other, weights, gate_mine, gate_other)
    took = send(give, swap)
    back = call(
        lambda *refs: pack_body(experts, capacity, *refs),
        sds((experts // 4, 4 * (capacity + 1) * tiles, LANES), bf16),
        "pack",
        [
            pltpu.VMEM((tiles, slots, LANES), f32),
            pltpu.VMEM((experts * (capacity + 1) * tiles, LANES), f32),
        ],
    )(keep, keep_gate, took)
    chunk = (capacity + 1) * tiles
    back = lax.all_to_all(
        back,
        "expert", split_axis=0, concat_axis=0, tiled=True, axis_index_groups=in_plane,
    )
    back = move(by_plane(back, chunk), home_perms)
    d_tokens, gate_grad = call(
        lambda *refs: combine_body(experts, capacity, *refs),
        (sds((tok_rows, width), bf16), sds((2, tok_rows), bf16)),
        "combine",
        [
            pltpu.VMEM((experts * (capacity + 1) * tiles, LANES), f32),
            pltpu.VMEM((tiles, slots, LANES), f32),
        ],
        1,
        6,
    )(plane, ids, gates_row, *back)
    d_tokens, gate_grad, total = lax.optimization_barrier((d_tokens, gate_grad, total))
    own = sds((width, shard), f32)
    grad_in, grad_out = call(finish_body, (own, own), "finish")(total)
    return d_tokens, gate_grad.T, grad_in[None], grad_out[None]


def solution(mesh):
    by_token = P(("dp", "expert"), None)
    by_expert = P("expert", None, "dp")
    return jax.shard_map(
        shards,
        mesh=mesh,
        in_specs=(by_token, by_token, by_token, by_token, by_expert, by_expert),
        out_specs=(by_token, by_token, by_expert, by_expert),
        check_vma=False,
    )
```
